32 devices in a mesh: parts: 2 (over x), grid: 8 (over z, y), depth: 2 (over core).
Axes of the slice: x: 2, y: 2, z: 4, core: 2. Of those that a mesh axis runs over, the one named last changes fastest.
Arguments:
- gate_input: bfloat16 [1024, 32768], P(('parts', 'depth'), 'grid'), parts along dimension 0, may hold values from -6 to 6
- up_input: bfloat16 [1024, 32768], P(('parts', 'depth'), 'grid'), parts along dimension 0, may hold values from -6 to 6
- code_values: bfloat16 [32768, 8192], P('grid', 'depth'), may hold values from -6 to 6, as said below
- exponents: int32 [1024, 8192], P('grid', 'depth'), may hold values from -10 to -7
- cotangent: bfloat16 [1024, 8192], P(('parts', 'depth'), 'grid'), parts along dimension 0, may hold values from -1.5 to 1.5
Outputs:
- output_rows: bfloat16 [1024, 8192], P(('parts', 'depth'), 'grid'), parts along dimension 0
- grad_gate: bfloat16 [1024, 32768], P(('parts', 'depth'), 'grid'), parts along dimension 0
- grad_up: bfloat16 [1024, 32768], P(('parts', 'depth'), 'grid'), parts along dimension 0
- grad_weight: bfloat16 [65536, 8192], P(('parts', 'grid'), 'depth'), parts along dimension 0
The draws below stay inside these ranges and needn't reach their ends.
There are 2 independent parts, one for each index of `parts`. The reference program is written for one: setup_inputs(seed, part) draws one part's arguments, and reference() takes and returns one part's arrays. A program takes and returns all parts, laid end to end along the dimension named above; an argument that names none is the same for every part. Nothing has to cross between parts.
Inputs may be any that keep to these rules, and one draw needn't show every extreme that they name: `code_values`: every entry is one of the E2M1 values 0, +-0.5, +-1, +-1.5, +-2, +-3, +-4, +-6.
All inputs are finite; a program needn't handle non-finite values.
Results may differ from the reference program's by a relative error of at most 0.0049.
Values may be sent and summed in bfloat16 or wider, within the bound.
A program may use at most 448 MiB of HBM per device.

```python
import jax
import jax.numpy as jnp

D = 8192
FFW = 32768
BLOCK = 32
TOKENS = 512


def draw_code_values(key, part):
    table = jnp.array([0.0, 0.5, 1.0, 1.5, 2.0, 3.0, 4.0, 6.0, 0.0, -0.5, -1.0, -1.5, -2.0, -3.0, -4.0, -6.0], jnp.float32)
    codes = jax.random.randint(jax.random.fold_in(key, 11), (FFW, D), 0, 16)
    return jnp.take(table, codes).astype(jnp.bfloat16)


def set_ends(values, rng, least, largest):
    spot = [jax.random.randint(jax.random.fold_in(rng, axis), (), 0, length) for axis, length in enumerate(values.shape)]
    widest = values.shape.index(max(values.shape))
    beside = spot[:widest] + [(spot[widest] + 1) % values.shape[widest]] + spot[widest + 1:]
    return values.at[tuple(spot)].set(least).at[tuple(beside)].set(largest)


def steps_of(rng, dims, cuts, least, largest):
    def one(dim, parts):
        heights = jax.random.uniform(jax.random.fold_in(jax.random.fold_in(rng, 6), dim), (parts,), jnp.float32, least / len(cuts), largest / len(cuts))
        return jnp.repeat(jnp.exp(heights), dims[dim] // parts).reshape((-1,) + (1,) * (len(dims) - dim - 1))

    gain = one(*cuts[0])
    for cut in cuts[1:]:
        gain = gain * one(*cut)
    return gain


def scatter_about(key, extent, deviation, bound, shards=(), kind=jnp.bfloat16):
    result = deviation * jax.random.normal(key, extent, jnp.float32)
    if shards:
        result = result * steps_of(key, extent, shards, -0.22, 0.18)
    return jnp.clip(result, -bound, bound).astype(kind)


def setup_inputs(seed: int = 0, part: int = 0) -> dict:
    splits = jax.random.split(jax.random.key(seed), 6)
    part_keys = jax.random.split(jax.random.fold_in(splits[5], part), 6)
    gate_input = scatter_about(part_keys[0], (TOKENS, FFW), 1.0, 6.0, ((0, 2), (1, 8)))
    up_input = scatter_about(part_keys[1], (TOKENS, FFW), 1.0, 6.0, ((0, 2), (1, 8)))
    code_values = draw_code_values(jax.random.fold_in(splits[5], 71), part)
    exponents = set_ends(jax.random.randint(splits[3], (FFW // BLOCK, D), -10, -6), jax.random.fold_in(splits[3], 1), -10, (-6) - 1).astype(jnp.int32)
    cotangent = scatter_about(part_keys[4], (TOKENS, D), 0.25, 1.5, ((0, 2), (1, 8)))
    return {"gate_input": gate_input, "up_input": up_input, "code_values": code_values, "exponents": exponents, "cotangent": cotangent}


def dequantize(code_values, exponents):
    scaled = jnp.exp2(exponents.astype(jnp.float32))
    blocks = code_values.astype(jnp.float32).reshape(FFW // BLOCK, BLOCK, D) * scaled[:, None, :]
    return blocks.reshape(FFW, D).astype(jnp.bfloat16)


def reference(gate_input, up_input, code_values, exponents, cotangent):
    weight = dequantize(code_values, exponents)
    gate_float = gate_input.astype(jnp.float32)
    up_float = up_input.astype(jnp.float32)
    sigmoid_gate = jax.nn.sigmoid(gate_float)
    activated = gate_float * sigmoid_gate
    hidden = (activated * up_float).astype(jnp.bfloat16)
    output_rows = jnp.dot(hidden, weight, preferred_element_type=jnp.float32).astype(jnp.bfloat16)
    grad_hidden = jnp.dot(cotangent, weight.T, preferred_element_type=jnp.float32)
    slope = sigmoid_gate * (1.0 + gate_float * (1.0 - sigmoid_gate))
    grad_gate = (grad_hidden * up_float * slope).astype(jnp.bfloat16)
    grad_up = (grad_hidden * activated).astype(jnp.bfloat16)
    grad_weight = jnp.dot(hidden.T, cotangent, preferred_element_type=jnp.float32).astype(jnp.bfloat16)
    return (output_rows, grad_gate, grad_up, grad_weight)
```

```python
import functools

import jax
import jax.numpy as jnp
from jax import lax
from jax.experimental import pallas as pl
from jax.experimental.pallas import tpu as pltpu
from jax.sharding import PartitionSpec as P

VMEM_LIMIT = 61 * 1024 * 1024
F32, BF16 = jnp.float32, jnp.bfloat16
MESH = pl.DeviceIdType.MESH
LAG = 2


def line_sizes(count):
    fast = 1
    while 4 * fast * fast <= count:
        fast *= 2
    return count // fast, fast


def tile(size, most):
    width = min(size, most)
    while size % width:
        width //= 2
    return width


def dequantized(codes, exponents):
    rows, columns = codes.shape
    scale = jnp.exp2(exponents.astype(F32)).astype(BF16)
    return (codes.reshape(rows // 32, 32, columns) * scale[:, None, :]).reshape(rows, columns)


class Plan:
    def __init__(self, slow, fast, tokens, columns, width):
        self.slow, self.fast, self.near = slow, fast, slow // 2
        self.tokens, self.total, self.columns, self.width = tokens, 2 * tokens, columns, width
        self.piece = tile(width, 512)
        self.parts = width // self.piece
        self.tiles = columns // self.piece
        self.cut = self.total * 5 // 8 // 16 * 16
        self.rows = (pl.ds(0, self.cut), pl.ds(self.cut, self.total - self.cut))

    def locate(self):
        grid, self.core = lax.axis_index("grid"), lax.axis_index("depth")
        self.y = grid % self.fast
        self.u = self.line(grid // self.fast)

    def line(self, place):
        return place + self.core * (self.slow - 1 - 2 * place)

    def grid_of(self, u, y):
        return self.line(u) * self.fast + y

    def index(self, owner, row, part):
        local = owner + self.core * (self.near - 1 - 2 * owner)
        return (local * self.fast + row) * self.parts + part

    def span(self, index):
        return pl.ds(pl.multiple_of(index * self.piece, self.piece), self.piece)

    def first_order(self, i):
        owner, rest = i // (self.fast * self.parts), i % (self.fast * self.parts)
        return owner, (self.y + 1 + rest // self.parts) % self.fast, rest % self.parts

    def second_order(self, i):
        step, rest = i // (self.fast * self.parts), i % (self.fast * self.parts)
        owner = (jnp.minimum(self.u, self.near - 1) - step + self.near) % self.near
        return owner, (self.y + rest // self.parts) % self.fast, rest % self.parts


def main_body(
    plan,
    gate_ref,
    up_ref,
    codes_ref,
    exponents_ref,
    cot_ref,
    hid_out,
    cot_out,
    mine_out,
    came_out,
    rows_out,
    hid,
    cots,
    part_sums,
    above,
    below,
    crossed,
    ended,
    sums,
    going,
    hid_send,
    hid_recv,
    hand_own,
    hand_send,
    hand_recv,
    gather_send,
    gather_recv,
    cross_send,
    cross_recv,
    end_send,
    end_recv,
    line_send,
    above_recv,
    below_recv,
    grad_send,
    grad_recv,
    rows_own,
    rows_send,
    rows_recv,
    save_sem,
    mine_sem,
):
    plan.locate()
    slow, fast, near, parts, tiles = plan.slow, plan.fast, plan.near, plan.parts, plan.tiles
    u, y, core, tokens = plan.u, plan.y, plan.core, plan.tokens
    step = pl.program_id(0)
    last = pl.num_programs(0) - 1
    units = hid.shape[1]
    own_rows = pl.ds(pl.multiple_of(core * tokens, tokens), tokens)
    other_rows = pl.ds(pl.multiple_of((1 - core) * tokens, tokens), tokens)

    def remote(source, target, send, recv, uu, yy, depth=None):
        place = plan.grid_of(uu, yy)
        return pltpu.make_async_remote_copy(
            src_ref=source,
            dst_ref=target,
            send_sem=send,
            recv_sem=recv,
            device_id={"grid": place, "depth": core if depth is None else depth},
            device_id_type=MESH,
        )

    def across_chip(source, target, send, recv):
        return pltpu.make_async_remote_copy(
            src_ref=source,
            dst_ref=target,
            send_sem=send,
            recv_sem=recv,
            device_id={"grid": lax.axis_index("grid"), "depth": 1 - core},
            device_id_type=MESH,
        )

    def wait_for(place, sem):
        pltpu.make_async_copy(place, place, sem).wait()

    def each(count, body):
        if count == 1:
            body(0)
        else:
            lax.fori_loop(0, count, lambda i, _: (body(i), 0)[1], 0)

    has_up, has_down = u < slow - 1, u > 0
    is_owner = u < near

    def greet():
        barrier = pltpu.get_barrier_semaphore()

        def hail(grid, depth):
            pl.semaphore_signal(barrier, inc=1, device_id={"grid": grid, "depth": depth}, device_id_type=MESH)

        @pl.when(has_up)
        def _():
            hail(plan.grid_of(u + 1, y), core)

        @pl.when(has_down)
        def _():
            hail(plan.grid_of(u - 1, y), core)

        for turn in range(1, fast):
            hail(plan.grid_of(u, (y + turn) % fast), core)
        hail(lax.axis_index("grid"), 1 - core)
        count = fast + has_up.astype(jnp.int32) + has_down.astype(jnp.int32)
        pl.semaphore_wait(barrier, count)

    def hand_piece(part):
        return cot_ref.at[:, plan.span(part)]

    def hand_over(part):
        owner = slow - 1 - u
        place = cots.at[own_rows, plan.span(_far_index(owner, part))]
        return across_chip(hand_piece(part), place, hand_send.at[part], hand_recv.at[part])

    def _far_index(owner, part):
        local = owner + (1 - core) * (near - 1 - 2 * owner)
        return (local * fast + y) * parts + part

    def keep_own(part):
        place = cots.at[own_rows, plan.span(plan.index(u, y, part))]
        return pltpu.make_async_copy(hand_piece(part), place, hand_own.at[part])

    def start_hand_over():
        @pl.when(is_owner)
        def _():
            for part in range(parts):
                keep_own(part).start()

        @pl.when(jnp.logical_not(is_owner))
        def _():
            for part in range(parts):
                hand_over(part).start()

    def block(kind, owner, row, part):
        return cots.at[plan.rows[kind], plan.span(plan.index(owner, row, part))]

    def gather_copy(kind, owner, row, part, way):
        index = plan.index(owner, row, part)
        place = block(kind, owner, row, part)
        uu, yy = (u + 1, y) if way == 0 else (u - 1, y) if way == 1 else (u, (y + way - 1) % fast)
        return remote(place, place, gather_send.at[kind, index, way], gather_recv.at[kind, index], uu, yy)

    def gather_ways(kind, owner, row, part, act):
        @pl.when(jnp.logical_and(u >= owner, has_up))
        def _():
            act(gather_copy(kind, owner, row, part, 0))

        @pl.when(jnp.logical_and(u <= owner, has_down))
        def _():
            act(gather_copy(kind, owner, row, part, 1))

        def over():
            for turn in range(1, fast):
                act(gather_copy(kind, owner, row, part, 1 + turn))

        if kind == 0:
            over()
        else:
            pl.when(jnp.logical_and(u == owner, row == y))(over)

    def start(copy):
        copy.start()

    def send_own(part):
        @pl.when(is_owner)
        def _():
            keep_own(part).wait()
            wait_for(cots.at[other_rows, plan.span(plan.index(u, y, part))], hand_recv.at[part])
            gather_ways(1, u, y, part, start)
            gather_ways(0, u, y, part, start)

    def pass_on(kind, owner, row, part):
        wait_for(block(kind, owner, row, part), gather_recv.at[kind, plan.index(owner, row, part)])
        gather_ways(kind, owner, row, part, start)

    def pass_crossed(part):
        @pl.when(is_owner)
        def _():
            each(fast - 1, lambda turn: pass_on(1, u, (y + 1 + turn) % fast, part))

    def pass_round(hop, part):
        for owner in (u - hop, u + hop):

            @pl.when(jnp.logical_and(owner >= 0, owner < near))
            def _():
                pass_on(0, owner, y, part)
                each(fast, lambda turn: pass_on(1, owner, (y + turn) % fast, part))

    def finish_gather():
        @pl.when(jnp.logical_not(is_owner))
        def _():
            for part in range(parts):
                hand_over(part).wait_send()

        def one(i):
            owner, rest = i // (fast * parts), i % (fast * parts)
            row, part = rest // parts, rest % parts

            @pl.when(row == y)
            def _():
                gather_ways(0, owner, row, part, lambda copy: copy.wait_send())

            gather_ways(1, owner, row, part, lambda copy: copy.wait_send())

        each(tiles, one)

    hid_parts = hid_send.shape[0]
    hid_width = units // hid_parts

    def hid_copy(i):
        place = hid.at[own_rows, pl.ds(pl.multiple_of(i * hid_width, hid_width), hid_width)]
        return across_chip(place, place, hid_send.at[i], hid_recv.at[i])

    def make_hidden(first, count):
        def one(i):
            columns = pl.ds(pl.multiple_of(i * hid_width, hid_width), hid_width)
            strip = min(32, tokens)

            def few(k, _):
                rows = pl.ds(pl.multiple_of(k * strip, strip), strip)
                gate = gate_ref[rows, columns].astype(F32)
                value = gate * jax.nn.sigmoid(gate) * up_ref[rows, columns].astype(F32)
                hid[pl.ds(pl.multiple_of(core * tokens + k * strip, strip), strip), columns] = value.astype(BF16)
                return 0

            lax.fori_loop(0, tokens // strip, few, 0)
            hid_copy(i).start()

        lax.fori_loop(first, first + count, lambda i, _: (one(i), 0)[1], 0)

    def hidden_arrives():
        def one(i):
            place = hid.at[other_rows, pl.ds(pl.multiple_of(i * hid_width, hid_width), hid_width)]
            wait_for(place, hid_recv.at[i])

        each(hid_parts, one)

    def out_piece(ref, kind, index):
        return ref.at[plan.rows[kind], plan.span(index)]

    def cross_place(owner, source, part):
        index = (source * near + owner) * parts + part
        return crossed.at[plan.rows[0], plan.span(index)], cross_recv.at[index]

    def cross_copy(owner, row, part):
        index = plan.index(owner, row, part)
        place, recv = cross_place(owner, y, part)
        return remote(out_piece(part_sums, 0, index), place, cross_send.at[index], recv, u, row)

    def end_place(source, part):
        index = source * parts + part
        return ended.at[:, plan.span(index)], end_recv.at[index]

    def end_copy(row, part):
        index = plan.index(u, row, part)
        place, recv = end_place(y, part)
        return remote(out_piece(part_sums, 1, index), place, end_send.at[index], recv, u, row)

    def line_copy(kind, owner, row, part, up):
        index = plan.index(owner, row, part)
        source = out_piece(part_sums, kind, index)
        if up:
            return remote(
                source, out_piece(below, kind, index), line_send.at[kind, index], below_recv.at[kind, index], u + 1, y
            )
        return remote(
            source, out_piece(above, kind, index), line_send.at[kind, index], above_recv.at[kind, index], u - 1, y
        )

    def add_into(kind, index, place):
        target = out_piece(part_sums, kind, index)
        target[...] = (target[...].astype(F32) + place[...].astype(F32)).astype(BF16)

    def take(kind, index, place, sem):
        wait_for(place, sem)
        add_into(kind, index, place)

    def line_event(owner, row, part):
        index = plan.index(owner, row, part)

        def one(kind):
            if kind == 0:

                def crossing(turn):
                    place, recv = cross_place(owner, (y + 1 + turn) % fast, part)
                    take(0, index, place, recv)

                each(fast - 1, crossing)

            @pl.when(jnp.logical_and(u >= owner, has_up))
            def _():
                take(kind, index, out_piece(above, kind, index), above_recv.at[kind, index])

            @pl.when(jnp.logical_and(u <= owner, has_down))
            def _():
                take(kind, index, out_piece(below, kind, index), below_recv.at[kind, index])

            @pl.when(u > owner)
            def _():
                line_copy(kind, owner, row, part, False).start()

            @pl.when(u < owner)
            def _():
                line_copy(kind, owner, row, part, True).start()

        pl.when(row == y)(lambda: one(0))
        one(1)

        @pl.when(jnp.logical_and(u == owner, row != y))
        def _():
            end_copy(row, part).start()

    def rows_copies(part):
        index = plan.index(u, y, part)
        target = rows_out.at[:, plan.span(part)]
        kept = pltpu.make_async_copy(part_sums.at[own_rows, plan.span(index)], target, rows_own.at[part])
        sent = across_chip(
            part_sums.at[other_rows, plan.span(index)], target, rows_send.at[part], rows_recv.at[part]
        )
        return kept, sent

    def final_event(row, part):
        @pl.when(row == y)
        def _():
            index = plan.index(u, y, part)

            def ending(turn):
                place, recv = end_place((y + 1 + turn) % fast, part)
                wait_for(place, recv)
                add_into(1, index, place)

            each(fast - 1, ending)
            for copy in rows_copies(part):
                copy.start()

    def sum_events():
        late, early = LAG * (slow - 1 - u), LAG * u

        def at(i, body):
            @pl.when(jnp.logical_and(i >= 0, i < tiles))
            def _():
                body(*plan.first_order(i))

        at(step - late, lambda owner, row, part: pl.when(owner <= u)(lambda: line_event(owner, row, part)))
        at(step - early, lambda owner, row, part: pl.when(owner > u)(lambda: line_event(owner, row, part)))
        at(step - late - LAG, lambda owner, row, part: pl.when(owner == u)(lambda: final_event(row, part)))

    def finish_sums():
        def one(i):
            owner, rest = i // (fast * parts), i % (fast * parts)
            row, part = rest // parts, rest % parts

            @pl.when(row != y)
            def _():
                cross_copy(owner, row, part).wait_send()

            for kind in range(2):

                def sent(kind=kind):
                    line_copy(kind, owner, row, part, True).wait_send()

                moved = u != owner
                pl.when(jnp.logical_and(moved, row == y) if kind == 0 else moved)(sent)

            @pl.when(jnp.logical_and(u == owner, row != y))
            def _():
                end_copy(row, part).wait_send()

        each(tiles, one)

        @pl.when(is_owner)
        def _():
            for part in range(parts):
                kept, sent = rows_copies(part)
                kept.wait()
                sent.wait_send()

        @pl.when(jnp.logical_not(is_owner))
        def _():
            for part in range(parts):
                wait_for(rows_out.at[:, plan.span(part)], rows_recv.at[part])

    slices = grad_send.shape[0]
    slice_width = units // slices

    def slice_of(i):
        return pl.ds(i * slice_width, slice_width)

    def grad_copy(i):
        return across_chip(going.at[:, slice_of(i)], came_out.at[:, slice_of(i)], grad_send.at[i], grad_recv.at[i])

    def mine_copy(i):
        return pltpu.make_async_copy(sums.at[own_rows, slice_of(i)], mine_out.at[:, slice_of(i)], mine_sem.at[i])

    def save(source, target, index):
        return pltpu.make_async_copy(source, target, save_sem.at[index])

    @pl.when(step == 0)
    def _():
        greet()
        start_hand_over()
        early = max(1, hid_parts // 4)
        make_hidden(0, early)
        for part in range(parts):
            send_own(part)
        make_hidden(early, hid_parts - early)
        hidden_arrives()
        save(hid, hid_out, 0).start()

    @pl.when(step == 1)
    def _():
        for part in range(parts):
            pass_crossed(part)

    whole = fast * parts
    for hop in range(1, slow):
        for part in range(parts):
            lead = slow - near
            if hop < lead:
                gap = tiles // lead
                when = hop * gap + part * (gap // parts)
            else:
                when = tiles + (hop - lead) * whole + part

            @pl.when(step == when)
            def _():
                pass_round(hop, part)

    @pl.when(step < tiles)
    def _():
        owner, row, part = plan.first_order(step)
        index = plan.index(owner, row, part)
        depth = tile(units, 1024)
        total = None
        for begin in range(0, units, depth):
            weight = dequantized(
                codes_ref[begin : begin + depth, :], exponents_ref[begin // 32 : (begin + depth) // 32, :]
            )
            term = jnp.dot(hid[:, begin : begin + depth], weight, preferred_element_type=F32)
            total = term if total is None else total + term
        part_sums[:, plan.span(index)] = total.astype(BF16)

        @pl.when(row != y)
        def _():
            cross_copy(owner, row, part).start()

    @pl.when(step >= tiles)
    def _():
        owner, row, part = plan.second_order(step - tiles)
        index = plan.index(owner, row, part)

        @pl.when(row != y)
        def _():
            wait_for(block(0, owner, row, part), gather_recv.at[0, index])

        def term_of(i):
            weight = dequantized(
                codes_ref[i * slice_width : (i + 1) * slice_width, :],
                exponents_ref[i * slice_width // 32 : (i + 1) * slice_width // 32, :],
            )
            return lax.dot_general(
                cots[:, plan.span(index)], weight, (((1,), (1,)), ((), ())), preferred_element_type=F32
            )

        @pl.when(step == tiles)
        def _():
            for i in range(slices):
                sums[:, slice_of(i)] = term_of(i)

        @pl.when(jnp.logical_and(step > tiles, step < last))
        def _():
            for i in range(slices):
                sums[:, slice_of(i)] += term_of(i)

        @pl.when(step == last)
        def _():
            save(cots, cot_out, 1).start()
            for i in range(slices):
                sums[:, slice_of(i)] += term_of(i)
                going[:, slice_of(i)] = sums[other_rows, slice_of(i)].astype(BF16)
                grad_copy(i).start()
                mine_copy(i).start()

    sum_events()

    @pl.when(step == last)
    def _():
        for i in range(slices):
            mine_copy(i).wait()
            grad_copy(i).wait()
        save(hid, hid_out, 0).wait()
        save(cots, cot_out, 1).wait()
        each(hid_parts, lambda i: hid_copy(i).wait_send())
        finish_gather()
        finish_sums()


def main_kernel(gate, up, codes, exponents, cotangent, slow, fast):
    tokens, units = gate.shape
    columns, width = codes.shape[1], cotangent.shape[1]
    plan = Plan(slow, fast, tokens, columns, width)
    tiles, parts, total, piece = plan.tiles, plan.parts, plan.total, plan.piece
    whole = pl.BlockSpec((tokens, units), lambda s: (0, 0), pipeline_mode=pl.Buffered(1))
    anywhere = pl.BlockSpec(memory_space=pl.ANY)
    dma = pltpu.SemaphoreType.DMA
    hid_parts = max(1, units // 512)
    slices = max(1, units // 512)

    def place(s):
        plan.locate()
        first = plan.index(*plan.first_order(jnp.minimum(s, tiles - 1)))
        second = plan.index(*plan.second_order(jnp.maximum(s - tiles, 0)))
        return jnp.where(s < tiles, first, second)

    return pl.pallas_call(
        functools.partial(main_body, plan),
        grid=(2 * tiles,),
        in_specs=[
            whole,
            whole,
            pl.BlockSpec((units, piece), lambda s: (0, place(s))),
            pl.BlockSpec((units // 32, piece), lambda s: (0, place(s))),
            anywhere,
        ],
        out_specs=[anywhere] * 5,
        out_shape=[
            jax.ShapeDtypeStruct((total, units), BF16),
            jax.ShapeDtypeStruct((total, columns), BF16),
            jax.ShapeDtypeStruct((tokens, units), F32),
            jax.ShapeDtypeStruct((tokens, units), BF16),
            jax.ShapeDtypeStruct((tokens, width), BF16),
        ],
        scratch_shapes=[
            pltpu.VMEM((total, units), BF16),
            pltpu.VMEM((total, columns), BF16),
            pltpu.VMEM((total, columns), BF16),
            pltpu.VMEM((total, columns), BF16),
            pltpu.VMEM((total, columns), BF16),
            pltpu.VMEM((plan.cut, columns), BF16),
            pltpu.VMEM((total - plan.cut, fast * width), BF16),
            pltpu.VMEM((total, units), F32),
            pltpu.VMEM((tokens, units), BF16),
            dma((hid_parts,)),
            dma((hid_parts,)),
            dma((parts,)),
            dma((parts,)),
            dma((parts,)),
            dma((2, tiles, 1 + fast)),
            dma((2, tiles)),
            dma((tiles,)),
            dma((tiles,)),
            dma((tiles,)),
            dma((fast * parts,)),
            dma((2, tiles)),
            dma((2, tiles)),
            dma((2, tiles)),
            dma((slices,)),
            dma((slices,)),
            dma((parts,)),
            dma((parts,)),
            dma((parts,)),
            dma((2,)),
            dma((slices,)),
        ],
        compiler_params=pltpu.CompilerParams(
            vmem_limit_bytes=VMEM_LIMIT, collective_id=0, has_side_effects=True
        ),
        cost_estimate=pl.CostEstimate(
            flops=8 * tokens * units * columns, bytes_accessed=4 * units * columns, transcendentals=0
        ),
        name="main",
    )(gate, up, codes, exponents, cotangent)


def weight_grad_body(width, hid_ref, cot_ref, out_ref):
    left = hid_ref[...].T
    for begin in range(0, out_ref.shape[1], width):
        term = jnp.dot(left, cot_ref[:, begin : begin + width], preferred_element_type=F32)
        out_ref[:, begin : begin + width] = term.astype(out_ref.dtype)


def weight_grad(hidden, cot_all):
    total, units = hidden.shape
    columns = cot_all.shape[1]
    height = tile(units, 512)
    return pl.pallas_call(
        functools.partial(weight_grad_body, tile(columns, 1024)),
        grid=(units // height,),
        in_specs=[
            pl.BlockSpec((total, height), lambda i: (0, i)),
            pl.BlockSpec((total, columns), lambda i: (0, 0), pipeline_mode=pl.Buffered(1)),
        ],
        out_specs=pl.BlockSpec((height, columns), lambda i: (i, 0)),
        out_shape=jax.ShapeDtypeStruct((units, columns), BF16),
        compiler_params=pltpu.CompilerParams(vmem_limit_bytes=VMEM_LIMIT),
        cost_estimate=pl.CostEstimate(
            flops=2 * total * units * columns, bytes_accessed=2 * units * columns, transcendentals=0
        ),
        name="weight_grad",
    )(hidden, cot_all)


def shards(slow, fast, gate_input, up_input, code_values, exponents, cotangent):
    hidden, cot_all, grad_mine, grad_came, output_rows = main_kernel(
        gate_input, up_input, code_values, exponents, cotangent, slow, fast
    )
    grad_weight = weight_grad(hidden, cot_all)
    gate_float = gate_input.astype(F32)
    up_float = up_input.astype(F32)
    sigmoid_gate = jax.nn.sigmoid(gate_float)
    activated = gate_float * sigmoid_gate
    grad_hidden = grad_mine + grad_came.astype(F32)
    slope = sigmoid_gate * (1.0 + gate_float * (1.0 - sigmoid_gate))
    grad_gate = (grad_hidden * up_float * slope).astype(BF16)
    grad_up = (grad_hidden * activated).astype(BF16)
    return (output_rows, grad_gate, grad_up, grad_weight)


def solution(mesh):
    tokens_units = P(("parts", "depth"), "grid")
    weights = P("grid", "depth")
    slow, fast = line_sizes(mesh.shape["grid"])
    return jax.shard_map(
        functools.partial(shards, slow, fast),
        mesh=mesh,
        in_specs=(tokens_units, tokens_units, weights, weights, tokens_units),
        out_specs=(tokens_units, tokens_units, tokens_units, P(("parts", "grid"), "depth")),
        check_vma=False,
    )
```

```python
import functools

import jax
import jax.numpy as jnp
from jax import lax
from jax.experimental import pallas as pl
from jax.experimental.pallas import tpu as pltpu
from jax.sharding import PartitionSpec as P

VMEM_LIMIT = 61 * 1024 * 1024
F32, BF16 = jnp.float32, jnp.bfloat16
MESH = pl.DeviceIdType.MESH
LAG = 2


def line_sizes(count):
    fast = 1
    while 4 * fast * fast <= count:
        fast *= 2
    return count // fast, fast


def tile(size, most):
    width = min(size, most)
    while size % width:
        width //= 2
    return width


def dequantized(codes, exponents):
    rows, columns = codes.shape
    scale = jnp.exp2(exponents.astype(F32)).astype(BF16)
    return (codes.reshape(rows // 32, 32, columns) * scale[:, None, :]).reshape(rows, columns)


class Plan:
    def __init__(self, slow, fast, tokens, columns, width):
        self.slow, self.fast, self.near = slow, fast, slow // 2
        self.tokens, self.total, self.columns, self.width = tokens, 2 * tokens, columns, width
        self.piece = tile(width, 512)
        self.parts = width // self.piece
        self.tiles = columns // self.piece
        self.cut = self.total * 5 // 8 // 16 * 16
        self.rows = (pl.ds(0, self.cut), pl.ds(self.cut, self.total - self.cut))

    def locate(self):
        grid, self.core = lax.axis_index("grid"), lax.axis_index("depth")
        self.y = grid % self.fast
        self.u = self.line(grid // self.fast)

    def line(self, place):
        return place + self.core * (self.slow - 1 - 2 * place)

    def grid_of(self, u, y):
        return self.line(u) * self.fast + y

    def index(self, owner, row, part):
        local = owner + self.core * (self.near - 1 - 2 * owner)
        return (local * self.fast + row) * self.parts + part

    def span(self, index):
        return pl.ds(pl.multiple_of(index * self.piece, self.piece), self.piece)

    def first_order(self, i):
        owner, rest = i // (self.fast * self.parts), i % (self.fast * self.parts)
        return owner, (self.y + 1 + rest // self.parts) % self.fast, rest % self.parts

    def second_order(self, i):
        step, rest = i // (self.fast * self.parts), i % (self.fast * self.parts)
        owner = (jnp.minimum(self.u, self.near - 1) - step + self.near) % self.near
        return owner, (self.y + rest // self.parts) % self.fast, rest % self.parts


def main_body(
    plan,
    gate_ref,
    up_ref,
    codes_ref,
    exponents_ref,
    cot_ref,
    hid_out,
    cot_out,
    mine_out,
    came_out,
    rows_out,
    hid,
    cots,
    part_sums,
    above,
    below,
    crossed,
    ended,
    sums,
    going,
    hid_send,
    hid_recv,
    hand_own,
    hand_send,
    hand_recv,
    gather_send,
    gather_recv,
    cross_send,
    cross_recv,
    end_send,
    end_recv,
    line_send,
    above_recv,
    below_recv,
    grad_send,
    grad_recv,
    rows_own,
    rows_send,
    rows_recv,
    save_sem,
    mine_sem,
):
    plan.locate()
    slow, fast, near, parts, tiles = plan.slow, plan.fast, plan.near, plan.parts, plan.tiles
    u, y, core, tokens = plan.u, plan.y, plan.core, plan.tokens
    step = pl.program_id(0)
    last = pl.num_programs(0) - 1
    units = hid.shape[1]
    own_rows = pl.ds(pl.multiple_of(core * tokens, tokens), tokens)
    other_rows = pl.ds(pl.multiple_of((1 - core) * tokens, tokens), tokens)

    def remote(source, target, send, recv, uu, yy, depth=None):
        place = plan.grid_of(uu, yy)
        return pltpu.make_async_remote_copy(
            src_ref=source,
            dst_ref=target,
            send_sem=send,
            recv_sem=recv,
            device_id={"grid": place, "depth": core if depth is None else depth},
            device_id_type=MESH,
        )

    def across_chip(source, target, send, recv):
        return pltpu.make_async_remote_copy(
            src_ref=source,
            dst_ref=target,
            send_sem=send,
            recv_sem=recv,
            device_id={"grid": lax.axis_index("grid"), "depth": 1 - core},
            device_id_type=MESH,
        )

    def wait_for(place, sem):
        pltpu.make_async_copy(place, place, sem).wait()

    def each(count, body):
        if count == 1:
            body(0)
        else:
            lax.fori_loop(0, count, lambda i, _: (body(i), 0)[1], 0)

    has_up, has_down = u < slow - 1, u > 0
    is_owner = u < near

    def greet():
        barrier = pltpu.get_barrier_semaphore()

        def hail(grid, depth):
            pl.semaphore_signal(barrier, inc=1, device_id={"grid": grid, "depth": depth}, device_id_type=MESH)

        @pl.when(has_up)
        def _():
            hail(plan.grid_of(u + 1, y), core)

        @pl.when(has_down)
        def _():
            hail(plan.grid_of(u - 1, y), core)

        for turn in range(1, fast):
            hail(plan.grid_of(u, (y + turn) % fast), core)
        hail(lax.axis_index("grid"), 1 - core)
        count = fast + has_up.astype(jnp.int32) + has_down.astype(jnp.int32)
        pl.semaphore_wait(barrier, count)

    def hand_piece(part):
        return cot_ref.at[:, plan.span(part)]

    def hand_over(part):
        owner = slow - 1 - u
        place = cots.at[own_rows, plan.span(_far_index(owner, part))]
        return across_chip(hand_piece(part), place, hand_send.at[part], hand_recv.at[part])

    def _far_index(owner, part):
        local = owner + (1 - core) * (near - 1 - 2 * owner)
        return (local * fast + y) * parts + part

    def keep_own(part):
        place = cots.at[own_rows, plan.span(plan.index(u, y, part))]
        return pltpu.make_async_copy(hand_piece(part), place, hand_own.at[part])

    def start_hand_over():
        @pl.when(is_owner)
        def _():
            for part in range(parts):
                keep_own(part).start()

        @pl.when(jnp.logical_not(is_owner))
        def _():
            for part in range(parts):
                hand_over(part).start()

    def block(kind, owner, row, part):
        return cots.at[plan.rows[kind], plan.span(plan.index(owner, row, part))]

    def gather_copy(kind, owner, row, part, way):
        index = plan.index(owner, row, part)
        place = block(kind, owner, row, part)
        uu, yy = (u + 1, y) if way == 0 else (u - 1, y) if way == 1 else (u, (y + way - 1) % fast)
        return remote(place, place, gather_send.at[kind, index, way], gather_recv.at[kind, index], uu, yy)

    def gather_ways(kind, owner, row, part, act):
        @pl.when(jnp.logical_and(u >= owner, has_up))
        def _():
            act(gather_copy(kind, owner, row, part, 0))

        @pl.when(jnp.logical_and(u <= owner, has_down))
        def _():
            act(gather_copy(kind, owner, row, part, 1))

        def over():
            for turn in range(1, fast):
                act(gather_copy(kind, owner, row, part, 1 + turn))

        if kind == 0:
            over()
        else:
            pl.when(jnp.logical_and(u == owner, row == y))(over)

    def start(copy):
        copy.start()

    def send_own(part):
        @pl.when(is_owner)
        def _():
            keep_own(part).wait()
            wait_for(cots.at[other_rows, plan.span(plan.index(u, y, part))], hand_recv.at[part])
            gather_ways(1, u, y, part, start)
            gather_ways(0, u, y, part, start)

    def pass_on(kind, owner, row, part):
        wait_for(block(kind, owner, row, part), gather_recv.at[kind, plan.index(owner, row, part)])
        gather_ways(kind, owner, row, part, start)

    def pass_crossed(part):
        @pl.when(is_owner)
        def _():
            each(fast - 1, lambda turn: pass_on(1, u, (y + 1 + turn) % fast, part))

    def pass_round(hop, part):
        for owner in (u - hop, u + hop):

            @pl.when(jnp.logical_and(owner >= 0, owner < near))
            def _():
                pass_on(0, owner, y, part)
                each(fast, lambda turn: pass_on(1, owner, (y + turn) % fast, part))

    def finish_gather():
        @pl.when(jnp.logical_not(is_owner))
        def _():
            for part in range(parts):
                hand_over(part).wait_send()

        def one(i):
            owner, rest = i // (fast * parts), i % (fast * parts)
            row, part = rest // parts, rest % parts

            @pl.when(row == y)
            def _():
                gather_ways(0, owner, row, part, lambda copy: copy.wait_send())

            gather_ways(1, owner, row, part, lambda copy: copy.wait_send())

        each(tiles, one)

    hid_parts = hid_send.shape[0]
    hid_width = units // hid_parts

    def hid_copy(i):
        place = hid.at[own_rows, pl.ds(pl.multiple_of(i * hid_width, hid_width), hid_width)]
        return across_chip(place, place, hid_send.at[i], hid_recv.at[i])

    def make_hidden(first, count):
        def one(i):
            columns = pl.ds(pl.multiple_of(i * hid_width, hid_width), hid_width)
            strip = min(32, tokens)

            def few(k, _):
                rows = pl.ds(pl.multiple_of(k * strip, strip), strip)
                gate = gate_ref[rows, columns].astype(F32)
                value = gate * jax.nn.sigmoid(gate) * up_ref[rows, columns].astype(F32)
                hid[pl.ds(pl.multiple_of(core * tokens + k * strip, strip), strip), columns] = value.astype(BF16)
                return 0

            lax.fori_loop(0, tokens // strip, few, 0)
            hid_copy(i).start()

        lax.fori_loop(first, first + count, lambda i, _: (one(i), 0)[1], 0)

    def hidden_arrives():
        def one(i):
            place = hid.at[other_rows, pl.ds(pl.multiple_of(i * hid_width, hid_width), hid_width)]
            wait_for(place, hid_recv.at[i])

        each(hid_parts, one)

    def out_piece(ref, kind, index):
        return ref.at[plan.rows[kind], plan.span(index)]

    def cross_place(owner, source, part):
        index = (source * near + owner) * parts + part
        return crossed.at[plan.rows[0], plan.span(index)], cross_recv.at[index]

    def cross_copy(owner, row, part):
        index = plan.index(owner, row, part)
        place, recv = cross_place(owner, y, part)
        return remote(out_piece(part_sums, 0, index), place, cross_send.at[index], recv, u, row)

    def end_place(source, part):
        index = source * parts + part
        return ended.at[:, plan.span(index)], end_recv.at[index]

    def end_copy(row, part):
        index = plan.index(u, row, part)
        place, recv = end_place(y, part)
        return remote(out_piece(part_sums, 1, index), place, end_send.at[index], recv, u, row)

    def line_copy(kind, owner, row, part, up):
        index = plan.index(owner, row, part)
        source = out_piece(part_sums, kind, index)
        if up:
            return remote(
                source, out_piece(below, kind, index), line_send.at[kind, index], below_recv.at[kind, index], u + 1, y
            )
        return remote(
            source, out_piece(above, kind, index), line_send.at[kind, index], above_recv.at[kind, index], u - 1, y
        )

    def combine(kind, index, places):
        for place, sem in places:
            wait_for(place, sem)
        target = out_piece(part_sums, kind, index)
        height = target.shape[0]
        strip = 32 if height % 32 == 0 else 16

        def few(k, _):
            rows = pl.ds(pl.multiple_of(k * strip, strip), strip)
            value = target[rows, :].astype(F32)
            for place, _ in places:
                value += place[rows, :].astype(F32)
            target[rows, :] = value.astype(BF16)
            return 0

        lax.fori_loop(0, height // strip, few, 0)

    def line_event(owner, row, part):
        index = plan.index(owner, row, part)

        def one(kind):
            crossing = [cross_place(owner, (y + turn) % fast, part) for turn in range(1, fast)] if kind == 0 else []
            from_above = out_piece(above, kind, index), above_recv.at[kind, index]
            from_below = out_piece(below, kind, index), below_recv.at[kind, index]
            takes_above = jnp.logical_and(u >= owner, has_up)
            takes_below = jnp.logical_and(u <= owner, has_down)

            @pl.when(jnp.logical_and(takes_above, takes_below))
            def _():
                combine(kind, index, [*crossing, from_above, from_below])

            @pl.when(jnp.logical_and(takes_above, jnp.logical_not(takes_below)))
            def _():
                combine(kind, index, [*crossing, from_above])

            @pl.when(jnp.logical_and(takes_below, jnp.logical_not(takes_above)))
            def _():
                combine(kind, index, [*crossing, from_below])

            if kind == 0:

                @pl.when(jnp.logical_not(jnp.logical_or(takes_above, takes_below)))
                def _():
                    combine(kind, index, crossing)

            @pl.when(u > owner)
            def _():
                line_copy(kind, owner, row, part, False).start()

            @pl.when(u < owner)
            def _():
                line_copy(kind, owner, row, part, True).start()

        pl.when(row == y)(lambda: one(0))
        one(1)

        @pl.when(jnp.logical_and(u == owner, row != y))
        def _():
            end_copy(row, part).start()

    def rows_copies(part):
        index = plan.index(u, y, part)
        target = rows_out.at[:, plan.span(part)]
        kept = pltpu.make_async_copy(part_sums.at[own_rows, plan.span(index)], target, rows_own.at[part])
        sent = across_chip(
            part_sums.at[other_rows, plan.span(index)], target, rows_send.at[part], rows_recv.at[part]
        )
        return kept, sent

    def final_event(row, part):
        @pl.when(row == y)
        def _():
            index = plan.index(u, y, part)
            combine(1, index, [end_place((y + turn) % fast, part) for turn in range(1, fast)])
            for copy in rows_copies(part):
                copy.start()

    def sum_events():
        late, early = LAG * (slow - 1 - u), LAG * u

        def at(i, body):
            @pl.when(jnp.logical_and(i >= 0, i < tiles))
            def _():
                body(*plan.first_order(i))

        at(step - late, lambda owner, row, part: pl.when(owner <= u)(lambda: line_event(owner, row, part)))
        at(step - early, lambda owner, row, part: pl.when(owner > u)(lambda: line_event(owner, row, part)))
        at(step - late - LAG, lambda owner, row, part: pl.when(owner == u)(lambda: final_event(row, part)))

    def finish_sums():
        def one(i):
            owner, rest = i // (fast * parts), i % (fast * parts)
            row, part = rest // parts, rest % parts

            @pl.when(row != y)
            def _():
                cross_copy(owner, row, part).wait_send()

            for kind in range(2):

                def sent(kind=kind):
                    line_copy(kind, owner, row, part, True).wait_send()

                moved = u != owner
                pl.when(jnp.logical_and(moved, row == y) if kind == 0 else moved)(sent)

            @pl.when(jnp.logical_and(u == owner, row != y))
            def _():
                end_copy(row, part).wait_send()

        each(tiles, one)

        @pl.when(is_owner)
        def _():
            for part in range(parts):
                kept, sent = rows_copies(part)
                kept.wait()
                sent.wait_send()

        @pl.when(jnp.logical_not(is_owner))
        def _():
            for part in range(parts):
                wait_for(rows_out.at[:, plan.span(part)], rows_recv.at[part])

    slices = grad_send.shape[0]
    slice_width = units // slices

    def slice_of(i):
        return pl.ds(i * slice_width, slice_width)

    def grad_copy(i):
        return across_chip(going.at[:, slice_of(i)], came_out.at[:, slice_of(i)], grad_send.at[i], grad_recv.at[i])

    def mine_copy(i):
        return pltpu.make_async_copy(sums.at[own_rows, slice_of(i)], mine_out.at[:, slice_of(i)], mine_sem.at[i])

    def save(source, target, index):
        return pltpu.make_async_copy(source, target, save_sem.at[index])

    @pl.when(step == 0)
    def _():
        greet()
        start_hand_over()
        early = max(1, hid_parts // 4)
        make_hidden(0, early)
        for part in range(parts):
            send_own(part)
        make_hidden(early, hid_parts - early)
        hidden_arrives()
        save(hid, hid_out, 0).start()

    @pl.when(step == 1)
    def _():
        for part in range(parts):
            pass_crossed(part)

    whole = fast * parts
    for hop in range(1, slow):
        for part in range(parts):
            lead = slow - near
            if hop < lead:
                gap = tiles // lead
                when = hop * gap + part * (gap // parts)
            else:
                when = tiles + (hop - lead) * whole + part

            @pl.when(step == when)
            def _():
                pass_round(hop, part)

    @pl.when(step < tiles)
    def _():
        owner, row, part = plan.first_order(step)
        index = plan.index(owner, row, part)
        depth = tile(units, 1024)
        total = None
        for begin in range(0, units, depth):
            weight = dequantized(
                codes_ref[begin : begin + depth, :], exponents_ref[begin // 32 : (begin + depth) // 32, :]
            )
            term = jnp.dot(hid[:, begin : begin + depth], weight, preferred_element_type=F32)
            total = term if total is None else total + term
        part_sums[:, plan.span(index)] = total.astype(BF16)

        @pl.when(row != y)
        def _():
            cross_copy(owner, row, part).start()

    @pl.when(step >= tiles)
    def _():
        owner, row, part = plan.second_order(step - tiles)
        index = plan.index(owner, row, part)

        @pl.when(row != y)
        def _():
            wait_for(block(0, owner, row, part), gather_recv.at[0, index])

        def term_of(i):
            weight = dequantized(
                codes_ref[i * slice_width : (i + 1) * slice_width, :],
                exponents_ref[i * slice_width // 32 : (i + 1) * slice_width // 32, :],
            )
            return lax.dot_general(
                cots[:, plan.span(index)], weight, (((1,), (1,)), ((), ())), preferred_element_type=F32
            )

        @pl.when(step == tiles)
        def _():
            for i in range(slices):
                sums[:, slice_of(i)] = term_of(i)

        @pl.when(jnp.logical_and(step > tiles, step < last))
        def _():
            for i in range(slices):
                sums[:, slice_of(i)] += term_of(i)

        @pl.when(step == last)
        def _():
            save(cots, cot_out, 1).start()
            for i in range(slices):
                sums[:, slice_of(i)] += term_of(i)
                going[:, slice_of(i)] = sums[other_rows, slice_of(i)].astype(BF16)
                grad_copy(i).start()
                mine_copy(i).start()

    sum_events()

    @pl.when(step == last)
    def _():
        for i in range(slices):
            mine_copy(i).wait()
            grad_copy(i).wait()
        save(hid, hid_out, 0).wait()
        save(cots, cot_out, 1).wait()
        each(hid_parts, lambda i: hid_copy(i).wait_send())
        finish_gather()
        finish_sums()


def main_kernel(gate, up, codes, exponents, cotangent, slow, fast):
    tokens, units = gate.shape
    columns, width = codes.shape[1], cotangent.shape[1]
    plan = Plan(slow, fast, tokens, columns, width)
    tiles, parts, total, piece = plan.tiles, plan.parts, plan.total, plan.piece
    whole = pl.BlockSpec((tokens, units), lambda s: (0, 0), pipeline_mode=pl.Buffered(1))
    anywhere = pl.BlockSpec(memory_space=pl.ANY)
    dma = pltpu.SemaphoreType.DMA
    hid_parts = max(1, units // 512)
    slices = max(1, units // 512)

    def place(s):
        plan.locate()
        first = plan.index(*plan.first_order(jnp.minimum(s, tiles - 1)))
        second = plan.index(*plan.second_order(jnp.maximum(s - tiles, 0)))
        return jnp.where(s < tiles, first, second)

    return pl.pallas_call(
        functools.partial(main_body, plan),
        grid=(2 * tiles,),
        in_specs=[
            whole,
            whole,
            pl.BlockSpec((units, piece), lambda s: (0, place(s))),
            pl.BlockSpec((units // 32, piece), lambda s: (0, place(s))),
            anywhere,
        ],
        out_specs=[anywhere] * 5,
        out_shape=[
            jax.ShapeDtypeStruct((total, units), BF16),
            jax.ShapeDtypeStruct((total, columns), BF16),
            jax.ShapeDtypeStruct((tokens, units), F32),
            jax.ShapeDtypeStruct((tokens, units), BF16),
            jax.ShapeDtypeStruct((tokens, width), BF16),
        ],
        scratch_shapes=[
            pltpu.VMEM((total, units), BF16),
            pltpu.VMEM((total, columns), BF16),
            pltpu.VMEM((total, columns), BF16),
            pltpu.VMEM((total, columns), BF16),
            pltpu.VMEM((total, columns), BF16),
            pltpu.VMEM((plan.cut, columns), BF16),
            pltpu.VMEM((total - plan.cut, fast * width), BF16),
            pltpu.VMEM((total, units), F32),
            pltpu.VMEM((tokens, units), BF16),
            dma((hid_parts,)),
            dma((hid_parts,)),
            dma((parts,)),
            dma((parts,)),
            dma((parts,)),
            dma((2, tiles, 1 + fast)),
            dma((2, tiles)),
            dma((tiles,)),
            dma((tiles,)),
            dma((tiles,)),
            dma((fast * parts,)),
            dma((2, tiles)),
            dma((2, tiles)),
            dma((2, tiles)),
            dma((slices,)),
            dma((slices,)),
            dma((parts,)),
            dma((parts,)),
            dma((parts,)),
            dma((2,)),
            dma((slices,)),
        ],
        compiler_params=pltpu.CompilerParams(
            vmem_limit_bytes=VMEM_LIMIT, collective_id=0, has_side_effects=True
        ),
        cost_estimate=pl.CostEstimate(
            flops=8 * tokens * units * columns, bytes_accessed=4 * units * columns, transcendentals=0
        ),
        name="main",
    )(gate, up, codes, exponents, cotangent)


def rest_body(
    width,
    gate_ref,
    up_ref,
    hid_ref,
    cot_ref,
    mine_ref,
    came_ref,
    rows_ref,
    grad_gate_ref,
    grad_up_ref,
    grad_weight_ref,
    rows_out_ref,
):
    @pl.when(pl.program_id(0) == 0)
    def _():
        rows_out_ref[...] = rows_ref[...]

    gate = gate_ref[...].astype(F32)
    sigmoid = jax.nn.sigmoid(gate)
    grad = mine_ref[...] + came_ref[...].astype(F32)
    slope = sigmoid * (1.0 + gate * (1.0 - sigmoid))
    grad_gate_ref[...] = (grad * up_ref[...].astype(F32) * slope).astype(BF16)
    grad_up_ref[...] = (grad * (gate * sigmoid)).astype(BF16)
    left = hid_ref[...].T
    for begin in range(0, grad_weight_ref.shape[1], width):
        term = jnp.dot(left, cot_ref[:, begin : begin + width], preferred_element_type=F32)
        grad_weight_ref[:, begin : begin + width] = term.astype(BF16)


def rest(gate, up, hidden, cot_all, grad_mine, grad_came, rows):
    total, units = hidden.shape
    tokens = gate.shape[0]
    columns = cot_all.shape[1]
    height = tile(units, 512)
    part = pl.BlockSpec((tokens, height), lambda i: (0, i))
    still = pl.BlockSpec(rows.shape, lambda i: (0, 0), pipeline_mode=pl.Buffered(1))
    return pl.pallas_call(
        functools.partial(rest_body, tile(columns, 1024)),
        grid=(units // height,),
        in_specs=[
            part,
            part,
            pl.BlockSpec((total, height), lambda i: (0, i)),
            pl.BlockSpec((total, columns), lambda i: (0, 0), pipeline_mode=pl.Buffered(1)),
            part,
            part,
            still,
        ],
        out_specs=[
            part,
            part,
            pl.BlockSpec((height, columns), lambda i: (i, 0)),
            pl.BlockSpec(rows.shape, lambda i: (0, 0)),
        ],
        out_shape=[
            jax.ShapeDtypeStruct((tokens, units), BF16),
            jax.ShapeDtypeStruct((tokens, units), BF16),
            jax.ShapeDtypeStruct((units, columns), BF16),
            jax.ShapeDtypeStruct(rows.shape, BF16),
        ],
        compiler_params=pltpu.CompilerParams(vmem_limit_bytes=VMEM_LIMIT),
        cost_estimate=pl.CostEstimate(
            flops=2 * total * units * columns, bytes_accessed=2 * units * columns, transcendentals=tokens * units
        ),
        name="rest",
    )(gate, up, hidden, cot_all, grad_mine, grad_came, rows)


def shards(slow, fast, gate_input, up_input, code_values, exponents, cotangent):
    hidden, cot_all, grad_mine, grad_came, rows = main_kernel(
        gate_input, up_input, code_values, exponents, cotangent, slow, fast
    )
    grad_gate, grad_up, grad_weight, output_rows = rest(
        gate_input, up_input, hidden, cot_all, grad_mine, grad_came, rows
    )
    return (output_rows, grad_gate, grad_up, grad_weight)


def solution(mesh):
    tokens_units = P(("parts", "depth"), "grid")
    weights = P("grid", "depth")
    slow, fast = line_sizes(mesh.shape["grid"])
    return jax.shard_map(
        functools.partial(shards, slow, fast),
        mesh=mesh,
        in_specs=(tokens_units, tokens_units, weights, weights, tokens_units),
        out_specs=(tokens_units, tokens_units, tokens_units, P(("parts", "grid"), "depth")),
        check_vma=False,
    )
```

```python
import functools

import jax
import jax.numpy as jnp
from jax import lax
from jax.experimental import pallas as pl
from jax.experimental.pallas import tpu as pltpu
from jax.sharding import PartitionSpec as P

VMEM_LIMIT = 61 * 1024 * 1024
F32, BF16 = jnp.float32, jnp.bfloat16
MESH = pl.DeviceIdType.MESH
LAG, DOWN_LAG, UP_LAG, END_LAG = 4, 2, 6, 2


def line_sizes(count):
    fast = 1
    while 4 * fast * fast <= count:
        fast *= 2
    return count // fast, fast


def tile(size, most):
    width = min(size, most)
    while size % width:
        width //= 2
    return width


def dequantized(codes, exponents):
    rows, columns = codes.shape
    scale = jnp.exp2(exponents.astype(F32)).astype(BF16)
    return (codes.reshape(rows // 32, 32, columns) * scale[:, None, :]).reshape(rows, columns)


class Plan:
    def __init__(self, slow, fast, tokens, columns, width):
        self.slow, self.fast, self.near = slow, fast, slow // 2
        self.tokens, self.total, self.columns, self.width = tokens, 2 * tokens, columns, width
        self.piece = tile(width, 512)
        self.parts = width // self.piece
        self.tiles = columns // self.piece
        self.cut = self.total * 9 // 16 // 16 * 16
        self.rows = (pl.ds(0, self.cut), pl.ds(self.cut, self.total - self.cut))

    def locate(self):
        grid, self.core = lax.axis_index("grid"), lax.axis_index("depth")
        self.y = grid % self.fast
        self.u = self.line(grid // self.fast)

    def line(self, place):
        return place + self.core * (self.slow - 1 - 2 * place)

    def grid_of(self, u, y):
        return self.line(u) * self.fast + y

    def index(self, owner, row, part):
        local = owner + self.core * (self.near - 1 - 2 * owner)
        return (local * self.fast + row) * self.parts + part

    def span(self, index):
        return pl.ds(pl.multiple_of(index * self.piece, self.piece), self.piece)

    def first_order(self, i):
        owner, rest = i // (self.fast * self.parts), i % (self.fast * self.parts)
        return owner, (self.y + 1 + rest // self.parts) % self.fast, rest % self.parts

    def second_order(self, i):
        step, rest = i // (self.fast * self.parts), i % (self.fast * self.parts)
        owner = (jnp.minimum(self.u, self.near - 1) - step + self.near) % self.near
        return owner, (self.y + rest // self.parts) % self.fast, rest % self.parts


def main_body(
    plan,
    gate_ref,
    up_ref,
    codes_ref,
    exponents_ref,
    cot_ref,
    hid_out,
    cot_out,
    mine_out,
    came_out,
    rows_out,
    hid,
    cots,
    part_sums,
    above,
    below,
    crossed,
    ended,
    sums,
    going,
    hid_send,
    hid_recv,
    hand_own,
    hand_send,
    hand_recv,
    gather_send,
    gather_recv,
    cross_send,
    cross_recv,
    end_send,
    end_recv,
    line_send,
    above_recv,
    below_recv,
    grad_send,
    grad_recv,
    rows_own,
    rows_send,
    rows_recv,
    save_sem,
    mine_sem,
):
    plan.locate()
    slow, fast, near, parts, tiles = plan.slow, plan.fast, plan.near, plan.parts, plan.tiles
    u, y, core, tokens = plan.u, plan.y, plan.core, plan.tokens
    step = pl.program_id(0)
    last = pl.num_programs(0) - 1
    units = hid.shape[1]
    own_rows = pl.ds(pl.multiple_of(core * tokens, tokens), tokens)
    other_rows = pl.ds(pl.multiple_of((1 - core) * tokens, tokens), tokens)

    def remote(source, target, send, recv, uu, yy, depth=None):
        place = plan.grid_of(uu, yy)
        return pltpu.make_async_remote_copy(
            src_ref=source,
            dst_ref=target,
            send_sem=send,
            recv_sem=recv,
            device_id={"grid": place, "depth": core if depth is None else depth},
            device_id_type=MESH,
        )

    def across_chip(source, target, send, recv):
        return pltpu.make_async_remote_copy(
            src_ref=source,
            dst_ref=target,
            send_sem=send,
            recv_sem=recv,
            device_id={"grid": lax.axis_index("grid"), "depth": 1 - core},
            device_id_type=MESH,
        )

    def wait_for(place, sem):
        pltpu.make_async_copy(place, place, sem).wait()

    def each(count, body):
        if count == 1:
            body(0)
        else:
            lax.fori_loop(0, count, lambda i, _: (body(i), 0)[1], 0)

    has_up, has_down = u < slow - 1, u > 0
    is_owner = u < near

    def greet():
        barrier = pltpu.get_barrier_semaphore()

        def hail(grid, depth):
            pl.semaphore_signal(barrier, inc=1, device_id={"grid": grid, "depth": depth}, device_id_type=MESH)

        @pl.when(has_up)
        def _():
            hail(plan.grid_of(u + 1, y), core)

        @pl.when(has_down)
        def _():
            hail(plan.grid_of(u - 1, y), core)

        for turn in range(1, fast):
            hail(plan.grid_of(u, (y + turn) % fast), core)
        hail(lax.axis_index("grid"), 1 - core)
        count = fast + has_up.astype(jnp.int32) + has_down.astype(jnp.int32)
        pl.semaphore_wait(barrier, count)

    def hand_piece(part):
        return cot_ref.at[:, plan.span(part)]

    def hand_over(part):
        owner = slow - 1 - u
        place = cots.at[own_rows, plan.span(_far_index(owner, part))]
        return across_chip(hand_piece(part), place, hand_send.at[part], hand_recv.at[part])

    def _far_index(owner, part):
        local = owner + (1 - core) * (near - 1 - 2 * owner)
        return (local * fast + y) * parts + part

    def keep_own(part):
        place = cots.at[own_rows, plan.span(plan.index(u, y, part))]
        return pltpu.make_async_copy(hand_piece(part), place, hand_own.at[part])

    def start_hand_over():
        @pl.when(is_owner)
        def _():
            for part in range(parts):
                keep_own(part).start()

        @pl.when(jnp.logical_not(is_owner))
        def _():
            for part in range(parts):
                hand_over(part).start()

    def block(kind, owner, row, part):
        return cots.at[plan.rows[kind], plan.span(plan.index(owner, row, part))]

    def gather_copy(kind, owner, row, part, way):
        index = plan.index(owner, row, part)
        place = block(kind, owner, row, part)
        uu, yy = (u + 1, y) if way == 0 else (u - 1, y) if way == 1 else (u, (y + way - 1) % fast)
        return remote(place, place, gather_send.at[kind, index, way], gather_recv.at[kind, index], uu, yy)

    def gather_ways(kind, owner, row, part, act):
        @pl.when(jnp.logical_and(u >= owner, has_up))
        def _():
            act(gather_copy(kind, owner, row, part, 0))

        @pl.when(jnp.logical_and(u <= owner, has_down))
        def _():
            act(gather_copy(kind, owner, row, part, 1))

        def over():
            for turn in range(1, fast):
                act(gather_copy(kind, owner, row, part, 1 + turn))

        if kind == 0:
            over()
        else:
            pl.when(jnp.logical_and(u == owner, row == y))(over)

    def start(copy):
        copy.start()

    def send_own(part):
        @pl.when(is_owner)
        def _():
            keep_own(part).wait()
            wait_for(cots.at[other_rows, plan.span(plan.index(u, y, part))], hand_recv.at[part])
            gather_ways(1, u, y, part, start)
            gather_ways(0, u, y, part, start)

    def pass_on(kind, owner, row, part):
        wait_for(block(kind, owner, row, part), gather_recv.at[kind, plan.index(owner, row, part)])
        gather_ways(kind, owner, row, part, start)

    def pass_crossed(part):
        @pl.when(is_owner)
        def _():
            each(fast - 1, lambda turn: pass_on(1, u, (y + 1 + turn) % fast, part))

    def pass_round(hop, part):
        for owner in (u - hop, u + hop):

            @pl.when(jnp.logical_and(owner >= 0, owner < near))
            def _():
                pass_on(0, owner, y, part)
                each(fast, lambda turn: pass_on(1, owner, (y + turn) % fast, part))

    def finish_gather():
        @pl.when(jnp.logical_not(is_owner))
        def _():
            for part in range(parts):
                hand_over(part).wait_send()

        def one(i):
            owner, rest = i // (fast * parts), i % (fast * parts)
            row, part = rest // parts, rest % parts

            @pl.when(row == y)
            def _():
                gather_ways(0, owner, row, part, lambda copy: copy.wait_send())

            gather_ways(1, owner, row, part, lambda copy: copy.wait_send())

        each(tiles, one)

    hid_parts = hid_send.shape[0]
    hid_width = units // hid_parts

    def hid_copy(i):
        place = hid.at[own_rows, pl.ds(pl.multiple_of(i * hid_width, hid_width), hid_width)]
        return across_chip(place, place, hid_send.at[i], hid_recv.at[i])

    def make_hidden(first, count):
        def one(i):
            columns = pl.ds(pl.multiple_of(i * hid_width, hid_width), hid_width)
            strip = min(32, tokens)

            def few(k, _):
                rows = pl.ds(pl.multiple_of(k * strip, strip), strip)
                gate = gate_ref[rows, columns].astype(F32)
                value = gate * jax.nn.sigmoid(gate) * up_ref[rows, columns].astype(F32)
                hid[pl.ds(pl.multiple_of(core * tokens + k * strip, strip), strip), columns] = value.astype(BF16)
                return 0

            lax.fori_loop(0, tokens // strip, few, 0)
            hid_copy(i).start()

        lax.fori_loop(first, first + count, lambda i, _: (one(i), 0)[1], 0)

    def hidden_arrives():
        def one(i):
            place = hid.at[other_rows, pl.ds(pl.multiple_of(i * hid_width, hid_width), hid_width)]
            wait_for(place, hid_recv.at[i])

        each(hid_parts, one)

    def out_piece(ref, kind, index):
        return ref.at[plan.rows[kind], plan.span(index)]

    def cross_place(owner, source, part):
        index = (source * near + owner) * parts + part
        return crossed.at[plan.rows[0], plan.span(index)], cross_recv.at[index]

    def cross_copy(owner, row, part):
        index = plan.index(owner, row, part)
        place, recv = cross_place(owner, y, part)
        return remote(out_piece(part_sums, 0, index), place, cross_send.at[index], recv, u, row)

    def end_place(source, part):
        index = source * parts + part
        return ended.at[:, plan.span(index)], end_recv.at[index]

    def end_copy(row, part):
        index = plan.index(u, row, part)
        place, recv = end_place(y, part)
        return remote(out_piece(part_sums, 1, index), place, end_send.at[index], recv, u, row)

    def line_copy(kind, owner, row, part, up):
        index = plan.index(owner, row, part)
        source = out_piece(part_sums, kind, index)
        if up:
            return remote(
                source, out_piece(below, kind, index), line_send.at[kind, index], below_recv.at[kind, index], u + 1, y
            )
        return remote(
            source, out_piece(above, kind, index), line_send.at[kind, index], above_recv.at[kind, index], u - 1, y
        )

    def combine(kind, index, places):
        for place, sem in places:
            wait_for(place, sem)
        target = out_piece(part_sums, kind, index)
        height = target.shape[0]
        strip = 32 if height % 32 == 0 else 16

        def few(k, _):
            rows = pl.ds(pl.multiple_of(k * strip, strip), strip)
            value = target[rows, :].astype(F32)
            for place, _ in places:
                value += place[rows, :].astype(F32)
            target[rows, :] = value.astype(BF16)
            return 0

        lax.fori_loop(0, height // strip, few, 0)

    def line_event(owner, row, part):
        index = plan.index(owner, row, part)

        def one(kind):
            crossing = [cross_place(owner, (y + turn) % fast, part) for turn in range(1, fast)] if kind == 0 else []
            from_above = out_piece(above, kind, index), above_recv.at[kind, index]
            from_below = out_piece(below, kind, index), below_recv.at[kind, index]
            takes_above = jnp.logical_and(u >= owner, has_up)
            takes_below = jnp.logical_and(u <= owner, has_down)

            @pl.when(jnp.logical_and(takes_above, takes_below))
            def _():
                combine(kind, index, [*crossing, from_above, from_below])

            @pl.when(jnp.logical_and(takes_above, jnp.logical_not(takes_below)))
            def _():
                combine(kind, index, [*crossing, from_above])

            @pl.when(jnp.logical_and(takes_below, jnp.logical_not(takes_above)))
            def _():
                combine(kind, index, [*crossing, from_below])

            if kind == 0:

                @pl.when(jnp.logical_not(jnp.logical_or(takes_above, takes_below)))
                def _():
                    combine(kind, index, crossing)

            @pl.when(u > owner)
            def _():
                line_copy(kind, owner, row, part, False).start()

            @pl.when(u < owner)
            def _():
                line_copy(kind, owner, row, part, True).start()

        pl.when(row == y)(lambda: one(0))
        one(1)

        @pl.when(jnp.logical_and(u == owner, row != y))
        def _():
            end_copy(row, part).start()

    def rows_copies(part):
        index = plan.index(u, y, part)
        target = rows_out.at[:, plan.span(part)]
        kept = pltpu.make_async_copy(part_sums.at[own_rows, plan.span(index)], target, rows_own.at[part])
        sent = across_chip(
            part_sums.at[other_rows, plan.span(index)], target, rows_send.at[part], rows_recv.at[part]
        )
        return kept, sent

    def final_event(row, part):
        @pl.when(row == y)
        def _():
            index = plan.index(u, y, part)
            combine(1, index, [end_place((y + turn) % fast, part) for turn in range(1, fast)])
            for copy in rows_copies(part):
                copy.start()

    def sum_events():
        down, up = DOWN_LAG + LAG * (slow - 1 - u), UP_LAG + LAG * u

        def at(lag, body):
            first = jnp.maximum(step - lag, 0)
            end = jnp.minimum(jnp.where(step == last, tiles, step - lag + 1), tiles)
            lax.fori_loop(first, end, lambda i, _: (body(*plan.first_order(i)), 0)[1], 0)

        at(up, lambda owner, row, part: pl.when(owner > u)(lambda: line_event(owner, row, part)))
        at(down, lambda owner, row, part: pl.when(owner <= u)(lambda: line_event(owner, row, part)))
        at(down + END_LAG, lambda owner, row, part: pl.when(owner == u)(lambda: final_event(row, part)))

    def finish_sums():
        def one(i):
            owner, rest = i // (fast * parts), i % (fast * parts)
            row, part = rest // parts, rest % parts

            @pl.when(row != y)
            def _():
                cross_copy(owner, row, part).wait_send()

            for kind in range(2):

                def sent(kind=kind):
                    line_copy(kind, owner, row, part, True).wait_send()

                moved = u != owner
                pl.when(jnp.logical_and(moved, row == y) if kind == 0 else moved)(sent)

            @pl.when(jnp.logical_and(u == owner, row != y))
            def _():
                end_copy(row, part).wait_send()

        each(tiles, one)

        @pl.when(is_owner)
        def _():
            for part in range(parts):
                kept, sent = rows_copies(part)
                kept.wait()
                sent.wait_send()

        @pl.when(jnp.logical_not(is_owner))
        def _():
            for part in range(parts):
                wait_for(rows_out.at[:, plan.span(part)], rows_recv.at[part])

    slices = grad_send.shape[0]
    slice_width = units // slices

    def slice_of(i):
        return pl.ds(i * slice_width, slice_width)

    def grad_copy(i):
        return across_chip(going.at[:, slice_of(i)], came_out.at[:, slice_of(i)], grad_send.at[i], grad_recv.at[i])

    def mine_copy(i):
        return pltpu.make_async_copy(sums.at[own_rows, slice_of(i)], mine_out.at[:, slice_of(i)], mine_sem.at[i])

    def save(source, target, index):
        return pltpu.make_async_copy(source, target, save_sem.at[index])

    @pl.when(step == 0)
    def _():
        greet()
        start_hand_over()
        early = max(1, hid_parts // 4)
        make_hidden(0, early)
        for part in range(parts):
            send_own(part)
        make_hidden(early, hid_parts - early)
        hidden_arrives()
        save(hid, hid_out, 0).start()

    @pl.when(step == 1)
    def _():
        for part in range(parts):
            pass_crossed(part)

    whole = fast * parts
    for hop in range(1, slow):
        for part in range(parts):
            lead = slow - near
            if hop < lead:
                when = max(1, hop * tiles // lead - 1) + part
            else:
                when = tiles + (hop - lead) * whole - min(hop - lead, 1) + part

            @pl.when(step == when)
            def _():
                pass_round(hop, part)

    @pl.when(step < tiles)
    def _():
        owner, row, part = plan.first_order(step)
        index = plan.index(owner, row, part)
        depth = tile(units, 1024)
        total = None
        for begin in range(0, units, depth):
            weight = dequantized(
                codes_ref[begin : begin + depth, :], exponents_ref[begin // 32 : (begin + depth) // 32, :]
            )
            term = jnp.dot(hid[:, begin : begin + depth], weight, preferred_element_type=F32)
            total = term if total is None else total + term
        part_sums[:, plan.span(index)] = total.astype(BF16)

        @pl.when(row != y)
        def _():
            cross_copy(owner, row, part).start()

    @pl.when(step >= tiles)
    def _():
        owner, row, part = plan.second_order(step - tiles)
        index = plan.index(owner, row, part)

        @pl.when(row != y)
        def _():
            wait_for(block(0, owner, row, part), gather_recv.at[0, index])

        def term_of(i):
            weight = dequantized(
                codes_ref[i * slice_width : (i + 1) * slice_width, :],
                exponents_ref[i * slice_width // 32 : (i + 1) * slice_width // 32, :],
            )
            return lax.dot_general(
                cots[:, plan.span(index)], weight, (((1,), (1,)), ((), ())), preferred_element_type=F32
            )

        @pl.when(step == tiles)
        def _():
            for i in range(slices):
                sums[:, slice_of(i)] = term_of(i)

        @pl.when(jnp.logical_and(step > tiles, step < last))
        def _():
            for i in range(slices):
                sums[:, slice_of(i)] += term_of(i)

        @pl.when(step == last)
        def _():
            save(cots, cot_out, 1).start()
            for i in range(slices):
                sums[:, slice_of(i)] += term_of(i)
                going[:, slice_of(i)] = sums[other_rows, slice_of(i)].astype(BF16)
                grad_copy(i).start()
                mine_copy(i).start()

    sum_events()

    @pl.when(step == last)
    def _():
        for i in range(slices):
            mine_copy(i).wait()
            grad_copy(i).wait()
        save(hid, hid_out, 0).wait()
        save(cots, cot_out, 1).wait()
        each(hid_parts, lambda i: hid_copy(i).wait_send())
        finish_gather()
        finish_sums()


def main_kernel(gate, up, codes, exponents, cotangent, slow, fast):
    tokens, units = gate.shape
    columns, width = codes.shape[1], cotangent.shape[1]
    plan = Plan(slow, fast, tokens, columns, width)
    tiles, parts, total, piece = plan.tiles, plan.parts, plan.total, plan.piece
    whole = pl.BlockSpec((tokens, units), lambda s: (0, 0), pipeline_mode=pl.Buffered(1))
    anywhere = pl.BlockSpec(memory_space=pl.ANY)
    dma = pltpu.SemaphoreType.DMA
    hid_parts = max(1, units // 512)
    slices = max(1, units // 512)

    def place(s):
        plan.locate()
        first = plan.index(*plan.first_order(jnp.minimum(s, tiles - 1)))
        second = plan.index(*plan.second_order(jnp.maximum(s - tiles, 0)))
        return jnp.where(s < tiles, first, second)

    return pl.pallas_call(
        functools.partial(main_body, plan),
        grid=(2 * tiles,),
        in_specs=[
            whole,
            whole,
            pl.BlockSpec((units, piece), lambda s: (0, place(s))),
            pl.BlockSpec((units // 32, piece), lambda s: (0, place(s))),
            anywhere,
        ],
        out_specs=[anywhere] * 5,
        out_shape=[
            jax.ShapeDtypeStruct((total, units), BF16),
            jax.ShapeDtypeStruct((total, columns), BF16),
            jax.ShapeDtypeStruct((tokens, units), F32),
            jax.ShapeDtypeStruct((tokens, units), BF16),
            jax.ShapeDtypeStruct((tokens, width), BF16),
        ],
        scratch_shapes=[
            pltpu.VMEM((total, units), BF16),
            pltpu.VMEM((total, columns), BF16),
            pltpu.VMEM((total, columns), BF16),
            pltpu.VMEM((total, columns), BF16),
            pltpu.VMEM((total, columns), BF16),
            pltpu.VMEM((plan.cut, columns), BF16),
            pltpu.VMEM((total - plan.cut, fast * width), BF16),
            pltpu.VMEM((total, units), F32),
            pltpu.VMEM((tokens, units), BF16),
            dma((hid_parts,)),
            dma((hid_parts,)),
            dma((parts,)),
            dma((parts,)),
            dma((parts,)),
            dma((2, tiles, 1 + fast)),
            dma((2, tiles)),
            dma((tiles,)),
            dma((tiles,)),
            dma((tiles,)),
            dma((fast * parts,)),
            dma((2, tiles)),
            dma((2, tiles)),
            dma((2, tiles)),
            dma((slices,)),
            dma((slices,)),
            dma((parts,)),
            dma((parts,)),
            dma((parts,)),
            dma((2,)),
            dma((slices,)),
        ],
        compiler_params=pltpu.CompilerParams(
            vmem_limit_bytes=VMEM_LIMIT, collective_id=0, has_side_effects=True
        ),
        cost_estimate=pl.CostEstimate(
            flops=8 * tokens * units * columns, bytes_accessed=4 * units * columns, transcendentals=0
        ),
        name="main",
    )(gate, up, codes, exponents, cotangent)


def rest_body(
    width,
    gate_ref,
    up_ref,
    hid_ref,
    cot_ref,
    mine_ref,
    came_ref,
    rows_ref,
    grad_gate_ref,
    grad_up_ref,
    grad_weight_ref,
    rows_out_ref,
):
    @pl.when(pl.program_id(0) == 0)
    def _():
        rows_out_ref[...] = rows_ref[...]

    gate = gate_ref[...].astype(F32)
    sigmoid = jax.nn.sigmoid(gate)
    grad = mine_ref[...] + came_ref[...].astype(F32)
    slope = sigmoid * (1.0 + gate * (1.0 - sigmoid))
    grad_gate_ref[...] = (grad * up_ref[...].astype(F32) * slope).astype(BF16)
    grad_up_ref[...] = (grad * (gate * sigmoid)).astype(BF16)
    left = hid_ref[...].T
    for begin in range(0, grad_weight_ref.shape[1], width):
        term = jnp.dot(left, cot_ref[:, begin : begin + width], preferred_element_type=F32)
        grad_weight_ref[:, begin : begin + width] = term.astype(BF16)


def rest(gate, up, hidden, cot_all, grad_mine, grad_came, rows):
    total, units = hidden.shape
    tokens = gate.shape[0]
    columns = cot_all.shape[1]
    height = tile(units, 512)
    part = pl.BlockSpec((tokens, height), lambda i: (0, i))
    still = pl.BlockSpec(rows.shape, lambda i: (0, 0), pipeline_mode=pl.Buffered(1))
    return pl.pallas_call(
        functools.partial(rest_body, tile(columns, 1024)),
        grid=(units // height,),
        in_specs=[
            part,
            part,
            pl.BlockSpec((total, height), lambda i: (0, i)),
            pl.BlockSpec((total, columns), lambda i: (0, 0), pipeline_mode=pl.Buffered(1)),
            part,
            part,
            still,
        ],
        out_specs=[
            part,
            part,
            pl.BlockSpec((height, columns), lambda i: (i, 0)),
            pl.BlockSpec(rows.shape, lambda i: (0, 0)),
        ],
        out_shape=[
            jax.ShapeDtypeStruct((tokens, units), BF16),
            jax.ShapeDtypeStruct((tokens, units), BF16),
            jax.ShapeDtypeStruct((units, columns), BF16),
            jax.ShapeDtypeStruct(rows.shape, BF16),
        ],
        compiler_params=pltpu.CompilerParams(vmem_limit_bytes=VMEM_LIMIT),
        cost_estimate=pl.CostEstimate(
            flops=2 * total * units * columns, bytes_accessed=2 * units * columns, transcendentals=tokens * units
        ),
        name="rest",
    )(gate, up, hidden, cot_all, grad_mine, grad_came, rows)


def shards(slow, fast, gate_input, up_input, code_values, exponents, cotangent):
    hidden, cot_all, grad_mine, grad_came, rows = main_kernel(
        gate_input, up_input, code_values, exponents, cotangent, slow, fast
    )
    grad_gate, grad_up, grad_weight, output_rows = rest(
        gate_input, up_input, hidden, cot_all, grad_mine, grad_came, rows
    )
    return (output_rows, grad_gate, grad_up, grad_weight)


def solution(mesh):
    tokens_units = P(("parts", "depth"), "grid")
    weights = P("grid", "depth")
    slow, fast = line_sizes(mesh.shape["grid"])
    return jax.shard_map(
        functools.partial(shards, slow, fast),
        mesh=mesh,
        in_specs=(tokens_units, tokens_units, weights, weights, tokens_units),
        out_specs=(tokens_units, tokens_units, tokens_units, P(("parts", "grid"), "depth")),
        check_vma=False,
    )
```

```python
import functools

import jax
import jax.numpy as jnp
from jax import lax
from jax.experimental import pallas as pl
from jax.experimental.pallas import tpu as pltpu
from jax.sharding import PartitionSpec as P

VMEM_LIMIT = 61 * 1024 * 1024
F32, BF16 = jnp.float32, jnp.bfloat16
MESH = pl.DeviceIdType.MESH
LAG, DOWN_LAG, UP_LAG, END_LAG = 4, 2, 6, 2


def line_sizes(count):
    fast = 1
    while 4 * fast * fast <= count:
        fast *= 2
    return count // fast, fast


def tile(size, most):
    width = min(size, most)
    while size % width:
        width //= 2
    return width


def dequantized(codes, exponents):
    rows, columns = codes.shape
    scale = jnp.exp2(exponents.astype(F32)).astype(BF16)
    return (codes.reshape(rows // 32, 32, columns) * scale[:, None, :]).reshape(rows, columns)


class Plan:
    def __init__(self, slow, fast, tokens, columns, width):
        self.slow, self.fast, self.near = slow, fast, slow // 2
        self.tokens, self.total, self.columns, self.width = tokens, 2 * tokens, columns, width
        self.piece = tile(width, 512)
        self.parts = width // self.piece
        self.tiles = columns // self.piece
        self.cut = self.total * 19 // 32 // 16 * 16
        self.rows = (pl.ds(0, self.cut), pl.ds(self.cut, self.total - self.cut))

    def locate(self):
        grid, self.core = lax.axis_index("grid"), lax.axis_index("depth")
        self.y = grid % self.fast
        self.u = self.line(grid // self.fast)

    def line(self, place):
        return place + self.core * (self.slow - 1 - 2 * place)

    def grid_of(self, u, y):
        return self.line(u) * self.fast + y

    def index(self, owner, row, part):
        local = owner + self.core * (self.near - 1 - 2 * owner)
        return (local * self.fast + row) * self.parts + part

    def span(self, index):
        return pl.ds(pl.multiple_of(index * self.piece, self.piece), self.piece)

    def first_order(self, i):
        owner, rest = i // (self.fast * self.parts), i % (self.fast * self.parts)
        return owner, (self.y + 1 + rest // self.parts) % self.fast, rest % self.parts

    def second_order(self, i):
        step, rest = i // (self.fast * self.parts), i % (self.fast * self.parts)
        owner = (jnp.minimum(self.u, self.near - 1) - step + self.near) % self.near
        return owner, (self.y + rest // self.parts) % self.fast, rest % self.parts


def main_body(
    plan,
    gate_in,
    up_in,
    codes_in,
    exponents_in,
    cot_ref,
    hid_out,
    cot_out,
    mine_out,
    came_out,
    rows_out,
    hid,
    cots,
    part_sums,
    above,
    below,
    crossed,
    ended,
    sums,
    going,
    hid_send,
    hid_recv,
    hand_own,
    hand_send,
    hand_recv,
    gather_send,
    gather_recv,
    cross_send,
    cross_recv,
    end_send,
    end_recv,
    line_send,
    above_recv,
    below_recv,
    grad_send,
    grad_recv,
    rows_own,
    rows_send,
    rows_recv,
    save_sem,
    mine_sem,
    gate_ref,
    up_ref,
    codes_slots,
    exponents_slots,
    gate_sem,
    up_sem,
    codes_sem,
    exponents_sem,
):
    plan.locate()
    slow, fast, near, parts, tiles = plan.slow, plan.fast, plan.near, plan.parts, plan.tiles
    u, y, core, tokens = plan.u, plan.y, plan.core, plan.tokens
    step = pl.program_id(0)
    last = pl.num_programs(0) - 1
    units = hid.shape[1]
    own_rows = pl.ds(pl.multiple_of(core * tokens, tokens), tokens)
    other_rows = pl.ds(pl.multiple_of((1 - core) * tokens, tokens), tokens)

    def remote(source, target, send, recv, uu, yy, depth=None):
        place = plan.grid_of(uu, yy)
        return pltpu.make_async_remote_copy(
            src_ref=source,
            dst_ref=target,
            send_sem=send,
            recv_sem=recv,
            device_id={"grid": place, "depth": core if depth is None else depth},
            device_id_type=MESH,
        )

    def across_chip(source, target, send, recv):
        return pltpu.make_async_remote_copy(
            src_ref=source,
            dst_ref=target,
            send_sem=send,
            recv_sem=recv,
            device_id={"grid": lax.axis_index("grid"), "depth": 1 - core},
            device_id_type=MESH,
        )

    def wait_for(place, sem):
        pltpu.make_async_copy(place, place, sem).wait()

    def each(count, body):
        if count == 1:
            body(0)
        else:
            lax.fori_loop(0, count, lambda i, _: (body(i), 0)[1], 0)

    has_up, has_down = u < slow - 1, u > 0
    is_owner = u < near

    def code_copies(at):
        first = plan.index(*plan.first_order(jnp.minimum(at, tiles - 1)))
        second = plan.index(*plan.second_order(jnp.maximum(at - tiles, 0)))
        span = plan.span(jnp.where(at < tiles, first, second))
        slot = at % 2
        return (
            pltpu.make_async_copy(codes_in.at[:, span], codes_slots.at[slot], codes_sem.at[slot]),
            pltpu.make_async_copy(exponents_in.at[:, span], exponents_slots.at[slot], exponents_sem.at[slot]),
        )

    def fetch(at):
        for copy in code_copies(at):
            copy.start()

    def branch_copies(i):
        columns = pl.ds(pl.multiple_of(i * hid_width, hid_width), hid_width)
        return (
            pltpu.make_async_copy(gate_in.at[:, columns], gate_ref.at[:, columns], gate_sem.at[i]),
            pltpu.make_async_copy(up_in.at[:, columns], up_ref.at[:, columns], up_sem.at[i]),
        )

    hid_parts = hid_send.shape[0]
    hid_width = units // hid_parts
    codes_ref, exponents_ref = codes_slots.at[step % 2], exponents_slots.at[step % 2]

    def greet():
        barrier = pltpu.get_barrier_semaphore()

        def hail(grid, depth):
            pl.semaphore_signal(barrier, inc=1, device_id={"grid": grid, "depth": depth}, device_id_type=MESH)

        @pl.when(has_up)
        def _():
            hail(plan.grid_of(u + 1, y), core)

        @pl.when(has_down)
        def _():
            hail(plan.grid_of(u - 1, y), core)

        for turn in range(1, fast):
            hail(plan.grid_of(u, (y + turn) % fast), core)
        hail(lax.axis_index("grid"), 1 - core)
        count = fast + has_up.astype(jnp.int32) + has_down.astype(jnp.int32)
        pl.semaphore_wait(barrier, count)

    def hand_piece(part):
        return cot_ref.at[:, plan.span(part)]

    def hand_over(part):
        owner = slow - 1 - u
        place = cots.at[own_rows, plan.span(_far_index(owner, part))]
        return across_chip(hand_piece(part), place, hand_send.at[part], hand_recv.at[part])

    def _far_index(owner, part):
        local = owner + (1 - core) * (near - 1 - 2 * owner)
        return (local * fast + y) * parts + part

    def keep_own(part):
        place = cots.at[own_rows, plan.span(plan.index(u, y, part))]
        return pltpu.make_async_copy(hand_piece(part), place, hand_own.at[part])

    def start_hand_over():
        @pl.when(is_owner)
        def _():
            for part in range(parts):
                keep_own(part).start()

        @pl.when(jnp.logical_not(is_owner))
        def _():
            for part in range(parts):
                hand_over(part).start()

    def block(kind, owner, row, part):
        return cots.at[plan.rows[kind], plan.span(plan.index(owner, row, part))]

    def gather_copy(kind, owner, row, part, way):
        index = plan.index(owner, row, part)
        place = block(kind, owner, row, part)
        uu, yy = (u + 1, y) if way == 0 else (u - 1, y) if way == 1 else (u, (y + way - 1) % fast)
        return remote(place, place, gather_send.at[kind, index, way], gather_recv.at[kind, index], uu, yy)

    def gather_ways(kind, owner, row, part, act):
        @pl.when(jnp.logical_and(u >= owner, has_up))
        def _():
            act(gather_copy(kind, owner, row, part, 0))

        @pl.when(jnp.logical_and(u <= owner, has_down))
        def _():
            act(gather_copy(kind, owner, row, part, 1))

        def over():
            for turn in range(1, fast):
                act(gather_copy(kind, owner, row, part, 1 + turn))

        if kind == 0:
            over()
        else:
            pl.when(jnp.logical_and(u == owner, row == y))(over)

    def start(copy):
        copy.start()

    def send_own(part):
        @pl.when(is_owner)
        def _():
            keep_own(part).wait()
            wait_for(cots.at[other_rows, plan.span(plan.index(u, y, part))], hand_recv.at[part])
            gather_ways(1, u, y, part, start)
            gather_ways(0, u, y, part, start)

    def pass_on(kind, owner, row, part):
        wait_for(block(kind, owner, row, part), gather_recv.at[kind, plan.index(owner, row, part)])
        gather_ways(kind, owner, row, part, start)

    def pass_crossed(part):
        @pl.when(is_owner)
        def _():
            each(fast - 1, lambda turn: pass_on(1, u, (y + 1 + turn) % fast, part))

    def pass_round(hop, part):
        for owner in (u - hop, u + hop):

            @pl.when(jnp.logical_and(owner >= 0, owner < near))
            def _():
                pass_on(0, owner, y, part)
                each(fast, lambda turn: pass_on(1, owner, (y + turn) % fast, part))

    def finish_gather():
        @pl.when(jnp.logical_not(is_owner))
        def _():
            for part in range(parts):
                hand_over(part).wait_send()

        def one(i):
            owner, rest = i // (fast * parts), i % (fast * parts)
            row, part = rest // parts, rest % parts

            @pl.when(row == y)
            def _():
                gather_ways(0, owner, row, part, lambda copy: copy.wait_send())

            gather_ways(1, owner, row, part, lambda copy: copy.wait_send())

        each(tiles, one)

    def hid_copy(i):
        place = hid.at[own_rows, pl.ds(pl.multiple_of(i * hid_width, hid_width), hid_width)]
        return across_chip(place, place, hid_send.at[i], hid_recv.at[i])

    def make_hidden(first, count):
        def one(i):
            columns = pl.ds(pl.multiple_of(i * hid_width, hid_width), hid_width)
            strip = min(32, tokens)
            for copy in branch_copies(i):
                copy.wait()

            def few(k, _):
                rows = pl.ds(pl.multiple_of(k * strip, strip), strip)
                gate = gate_ref[rows, columns].astype(F32)
                value = gate * jax.nn.sigmoid(gate) * up_ref[rows, columns].astype(F32)
                hid[pl.ds(pl.multiple_of(core * tokens + k * strip, strip), strip), columns] = value.astype(BF16)
                return 0

            lax.fori_loop(0, tokens // strip, few, 0, unroll=min(4, tokens // strip))
            hid_copy(i).start()

        lax.fori_loop(first, first + count, lambda i, _: (one(i), 0)[1], 0)

    def hidden_arrives():
        def one(i):
            place = hid.at[other_rows, pl.ds(pl.multiple_of(i * hid_width, hid_width), hid_width)]
            wait_for(place, hid_recv.at[i])

        each(hid_parts, one)

    def out_piece(ref, kind, index):
        return ref.at[plan.rows[kind], plan.span(index)]

    def cross_place(owner, source, part):
        index = (source * near + owner) * parts + part
        return crossed.at[plan.rows[0], plan.span(index)], cross_recv.at[index]

    def cross_copy(owner, row, part):
        index = plan.index(owner, row, part)
        place, recv = cross_place(owner, y, part)
        return remote(out_piece(part_sums, 0, index), place, cross_send.at[index], recv, u, row)

    def end_place(source, part):
        index = source * parts + part
        return ended.at[:, plan.span(index)], end_recv.at[index]

    def end_copy(row, part):
        index = plan.index(u, row, part)
        place, recv = end_place(y, part)
        return remote(out_piece(part_sums, 1, index), place, end_send.at[index], recv, u, row)

    def line_copy(kind, owner, row, part, up):
        index = plan.index(owner, row, part)
        source = out_piece(part_sums, kind, index)
        if up:
            return remote(
                source, out_piece(below, kind, index), line_send.at[kind, index], below_recv.at[kind, index], u + 1, y
            )
        return remote(
            source, out_piece(above, kind, index), line_send.at[kind, index], above_recv.at[kind, index], u - 1, y
        )

    def combine(kind, index, places):
        for place, sem in places:
            wait_for(place, sem)
        target = out_piece(part_sums, kind, index)
        height = target.shape[0]
        strip = 32 if height % 32 == 0 else 16

        def few(k, _):
            rows = pl.ds(pl.multiple_of(k * strip, strip), strip)
            value = target[rows, :].astype(F32)
            for place, _ in places:
                value += place[rows, :].astype(F32)
            target[rows, :] = value.astype(BF16)
            return 0

        lax.fori_loop(0, height // strip, few, 0)

    def line_event(owner, row, part):
        index = plan.index(owner, row, part)

        def one(kind):
            crossing = [cross_place(owner, (y + turn) % fast, part) for turn in range(1, fast)] if kind == 0 else []
            from_above = out_piece(above, kind, index), above_recv.at[kind, index]
            from_below = out_piece(below, kind, index), below_recv.at[kind, index]
            takes_above = jnp.logical_and(u >= owner, has_up)
            takes_below = jnp.logical_and(u <= owner, has_down)

            @pl.when(jnp.logical_and(takes_above, takes_below))
            def _():
                combine(kind, index, [*crossing, from_above, from_below])

            @pl.when(jnp.logical_and(takes_above, jnp.logical_not(takes_below)))
            def _():
                combine(kind, index, [*crossing, from_above])

            @pl.when(jnp.logical_and(takes_below, jnp.logical_not(takes_above)))
            def _():
                combine(kind, index, [*crossing, from_below])

            if kind == 0:

                @pl.when(jnp.logical_not(jnp.logical_or(takes_above, takes_below)))
                def _():
                    combine(kind, index, crossing)

            @pl.when(u > owner)
            def _():
                line_copy(kind, owner, row, part, False).start()

            @pl.when(u < owner)
            def _():
                line_copy(kind, owner, row, part, True).start()

        pl.when(row == y)(lambda: one(0))
        one(1)

        @pl.when(jnp.logical_and(u == owner, row != y))
        def _():
            end_copy(row, part).start()

    def rows_copies(part):
        index = plan.index(u, y, part)
        target = rows_out.at[:, plan.span(part)]
        kept = pltpu.make_async_copy(part_sums.at[own_rows, plan.span(index)], target, rows_own.at[part])
        sent = across_chip(
            part_sums.at[other_rows, plan.span(index)], target, rows_send.at[part], rows_recv.at[part]
        )
        return kept, sent

    def final_event(row, part):
        @pl.when(row == y)
        def _():
            index = plan.index(u, y, part)
            combine(1, index, [end_place((y + turn) % fast, part) for turn in range(1, fast)])
            for copy in rows_copies(part):
                copy.start()

    def sum_events():
        down, up = DOWN_LAG + LAG * (slow - 1 - u), UP_LAG + LAG * u

        def at(lag, body):
            first = jnp.maximum(step - lag, 0)
            end = jnp.minimum(jnp.where(step == last, tiles, step - lag + 1), tiles)
            lax.fori_loop(first, end, lambda i, _: (body(*plan.first_order(i)), 0)[1], 0)

        at(up, lambda owner, row, part: pl.when(owner > u)(lambda: line_event(owner, row, part)))
        at(down, lambda owner, row, part: pl.when(owner <= u)(lambda: line_event(owner, row, part)))
        at(down + END_LAG, lambda owner, row, part: pl.when(owner == u)(lambda: final_event(row, part)))

    def finish_sums():
        def one(i):
            owner, rest = i // (fast * parts), i % (fast * parts)
            row, part = rest // parts, rest % parts

            @pl.when(row != y)
            def _():
                cross_copy(owner, row, part).wait_send()

            for kind in range(2):

                def sent(kind=kind):
                    line_copy(kind, owner, row, part, True).wait_send()

                moved = u != owner
                pl.when(jnp.logical_and(moved, row == y) if kind == 0 else moved)(sent)

            @pl.when(jnp.logical_and(u == owner, row != y))
            def _():
                end_copy(row, part).wait_send()

        each(tiles, one)

        @pl.when(is_owner)
        def _():
            for part in range(parts):
                kept, sent = rows_copies(part)
                kept.wait()
                sent.wait_send()

        @pl.when(jnp.logical_not(is_owner))
        def _():
            for part in range(parts):
                wait_for(rows_out.at[:, plan.span(part)], rows_recv.at[part])

    slices = grad_send.shape[0]
    slice_width = units // slices

    def slice_of(i):
        return pl.ds(i * slice_width, slice_width)

    def grad_copy(i):
        return across_chip(going.at[:, slice_of(i)], came_out.at[:, slice_of(i)], grad_send.at[i], grad_recv.at[i])

    def mine_copy(i):
        return pltpu.make_async_copy(sums.at[own_rows, slice_of(i)], mine_out.at[:, slice_of(i)], mine_sem.at[i])

    def save(source, target, index):
        return pltpu.make_async_copy(source, target, save_sem.at[index])

    @pl.when(step == 0)
    def _():
        for i in range(hid_parts):
            for copy in branch_copies(i):
                copy.start()
        fetch(step)
        greet()
        start_hand_over()
        early = max(1, hid_parts // 8)
        make_hidden(0, early)
        for part in range(parts):
            send_own(part)
        make_hidden(early, hid_parts - early)
        hidden_arrives()
        save(hid, hid_out, 0).start()

    @pl.when(step == 1)
    def _():
        for part in range(parts):
            pass_crossed(part)

    @pl.when(step < last)
    def _():
        fetch(step + 1)

    whole = fast * parts
    for hop in range(1, slow):
        for part in range(parts):
            lead = slow - near
            if hop < lead:
                when = max(1, hop * tiles // lead - 1) + part
            else:
                when = tiles + (hop - lead) * whole - min(hop - lead, 1) + part

            @pl.when(step == when)
            def _():
                pass_round(hop, part)

    for copy in code_copies(step):
        copy.wait()

    @pl.when(step < tiles)
    def _():
        owner, row, part = plan.first_order(step)
        index = plan.index(owner, row, part)
        depth = tile(units, 1024)
        total = None
        for begin in range(0, units, depth):
            weight = dequantized(
                codes_ref[begin : begin + depth, :], exponents_ref[begin // 32 : (begin + depth) // 32, :]
            )
            term = jnp.dot(hid[:, begin : begin + depth], weight, preferred_element_type=F32)
            total = term if total is None else total + term
        part_sums[:, plan.span(index)] = total.astype(BF16)

        @pl.when(row != y)
        def _():
            cross_copy(owner, row, part).start()

    @pl.when(step >= tiles)
    def _():
        owner, row, part = plan.second_order(step - tiles)
        index = plan.index(owner, row, part)

        @pl.when(row != y)
        def _():
            wait_for(block(0, owner, row, part), gather_recv.at[0, index])

        def term_of(i):
            weight = dequantized(
                codes_ref[i * slice_width : (i + 1) * slice_width, :],
                exponents_ref[i * slice_width // 32 : (i + 1) * slice_width // 32, :],
            )
            return lax.dot_general(
                cots[:, plan.span(index)], weight, (((1,), (1,)), ((), ())), preferred_element_type=F32
            )

        @pl.when(step == tiles)
        def _():
            for i in range(slices):
                sums[:, slice_of(i)] = term_of(i)

        @pl.when(jnp.logical_and(step > tiles, step < last))
        def _():
            for i in range(slices):
                sums[:, slice_of(i)] += term_of(i)

        @pl.when(step == last)
        def _():
            save(cots, cot_out, 1).start()
            for i in range(slices):
                sums[:, slice_of(i)] += term_of(i)
                going[:, slice_of(i)] = sums[other_rows, slice_of(i)].astype(BF16)
                grad_copy(i).start()
                mine_copy(i).start()

    sum_events()

    @pl.when(step == last)
    def _():
        for i in range(slices):
            mine_copy(i).wait()
            grad_copy(i).wait()
        save(hid, hid_out, 0).wait()
        save(cots, cot_out, 1).wait()
        each(hid_parts, lambda i: hid_copy(i).wait_send())
        finish_gather()
        finish_sums()


def main_kernel(gate, up, codes, exponents, cotangent, slow, fast):
    tokens, units = gate.shape
    columns, width = codes.shape[1], cotangent.shape[1]
    plan = Plan(slow, fast, tokens, columns, width)
    tiles, parts, total, piece = plan.tiles, plan.parts, plan.total, plan.piece
    anywhere = pl.BlockSpec(memory_space=pl.ANY)
    dma = pltpu.SemaphoreType.DMA
    hid_parts = max(1, units // 512)
    slices = max(1, units // 512)

    return pl.pallas_call(
        functools.partial(main_body, plan),
        grid=(2 * tiles,),
        in_specs=[anywhere] * 5,
        out_specs=[anywhere] * 5,
        out_shape=[
            jax.ShapeDtypeStruct((total, units), BF16),
            jax.ShapeDtypeStruct((total, columns), BF16),
            jax.ShapeDtypeStruct((tokens, units), F32),
            jax.ShapeDtypeStruct((tokens, units), BF16),
            jax.ShapeDtypeStruct((tokens, width), BF16),
        ],
        scratch_shapes=[
            pltpu.VMEM((total, units), BF16),
            pltpu.VMEM((total, columns), BF16),
            pltpu.VMEM((total, columns), BF16),
            pltpu.VMEM((total, columns), BF16),
            pltpu.VMEM((total, columns), BF16),
            pltpu.VMEM((plan.cut, columns), BF16),
            pltpu.VMEM((total - plan.cut, fast * width), BF16),
            pltpu.VMEM((total, units), F32),
            pltpu.VMEM((tokens, units), BF16),
            dma((hid_parts,)),
            dma((hid_parts,)),
            dma((parts,)),
            dma((parts,)),
            dma((parts,)),
            dma((2, tiles, 1 + fast)),
            dma((2, tiles)),
            dma((tiles,)),
            dma((tiles,)),
            dma((tiles,)),
            dma((fast * parts,)),
            dma((2, tiles)),
            dma((2, tiles)),
            dma((2, tiles)),
            dma((slices,)),
            dma((slices,)),
            dma((parts,)),
            dma((parts,)),
            dma((parts,)),
            dma((2,)),
            dma((slices,)),
            pltpu.VMEM((tokens, units), BF16),
            pltpu.VMEM((tokens, units), BF16),
            pltpu.VMEM((2, units, piece), BF16),
            pltpu.VMEM((2, units // 32, piece), jnp.int32),
            dma((hid_parts,)),
            dma((hid_parts,)),
            dma((2,)),
            dma((2,)),
        ],
        compiler_params=pltpu.CompilerParams(
            vmem_limit_bytes=VMEM_LIMIT, collective_id=0, has_side_effects=True
        ),
        cost_estimate=pl.CostEstimate(
            flops=8 * tokens * units * columns, bytes_accessed=4 * units * columns, transcendentals=0
        ),
        name="main",
    )(gate, up, codes, exponents, cotangent)


def rest_body(
    width,
    gate_ref,
    up_ref,
    hid_ref,
    cot_ref,
    mine_ref,
    came_ref,
    rows_ref,
    grad_gate_ref,
    grad_up_ref,
    grad_weight_ref,
    rows_out_ref,
):
    @pl.when(pl.program_id(0) == 0)
    def _():
        rows_out_ref[...] = rows_ref[...]

    left = hid_ref[...].T
    columns, tokens = grad_weight_ref.shape[1], gate_ref.shape[0]
    height = tokens * width // columns
    for i in range(columns // width):
        rows, begin = slice(i * height, (i + 1) * height), i * width
        gate = gate_ref[rows, :].astype(F32)
        sigmoid = jax.nn.sigmoid(gate)
        grad = mine_ref[rows, :] + came_ref[rows, :].astype(F32)
        slope = sigmoid * (1.0 + gate * (1.0 - sigmoid))
        grad_gate = (grad * up_ref[rows, :].astype(F32) * slope).astype(BF16)
        grad_up = (grad * (gate * sigmoid)).astype(BF16)
        term = jnp.dot(left, cot_ref[:, begin : begin + width], preferred_element_type=F32)
        grad_weight_ref[:, begin : begin + width] = term.astype(BF16)
        grad_gate_ref[rows, :] = grad_gate
        grad_up_ref[rows, :] = grad_up


def rest(gate, up, hidden, cot_all, grad_mine, grad_came, rows):
    total, units = hidden.shape
    tokens = gate.shape[0]
    columns = cot_all.shape[1]
    height = tile(units, 512)
    part = pl.BlockSpec((tokens, height), lambda i: (0, i))
    still = pl.BlockSpec(rows.shape, lambda i: (0, 0), pipeline_mode=pl.Buffered(1))
    return pl.pallas_call(
        functools.partial(rest_body, tile(columns, 1024)),
        grid=(units // height,),
        in_specs=[
            part,
            part,
            pl.BlockSpec((total, height), lambda i: (0, i)),
            pl.BlockSpec((total, columns), lambda i: (0, 0), pipeline_mode=pl.Buffered(1)),
            part,
            part,
            still,
        ],
        out_specs=[
            part,
            part,
            pl.BlockSpec((height, columns), lambda i: (i, 0)),
            pl.BlockSpec(rows.shape, lambda i: (0, 0)),
        ],
        out_shape=[
            jax.ShapeDtypeStruct((tokens, units), BF16),
            jax.ShapeDtypeStruct((tokens, units), BF16),
            jax.ShapeDtypeStruct((units, columns), BF16),
            jax.ShapeDtypeStruct(rows.shape, BF16),
        ],
        compiler_params=pltpu.CompilerParams(vmem_limit_bytes=VMEM_LIMIT),
        cost_estimate=pl.CostEstimate(
            flops=2 * total * units * columns, bytes_accessed=2 * units * columns, transcendentals=tokens * units
        ),
        name="rest",
    )(gate, up, hidden, cot_all, grad_mine, grad_came, rows)


def shards(slow, fast, gate_input, up_input, code_values, exponents, cotangent):
    hidden, cot_all, grad_mine, grad_came, rows = main_kernel(
        gate_input, up_input, code_values, exponents, cotangent, slow, fast
    )
    grad_gate, grad_up, grad_weight, output_rows = rest(
        gate_input, up_input, hidden, cot_all, grad_mine, grad_came, rows
    )
    return (output_rows, grad_gate, grad_up, grad_weight)


def solution(mesh):
    tokens_units = P(("parts", "depth"), "grid")
    weights = P("grid", "depth")
    slow, fast = line_sizes(mesh.shape["grid"])
    return jax.shard_map(
        functools.partial(shards, slow, fast),
        mesh=mesh,
        in_specs=(tokens_units, tokens_units, weights, weights, tokens_units),
        out_specs=(tokens_units, tokens_units, tokens_units, P(("parts", "grid"), "depth")),
        check_vma=False,
    )
```

```python
import functools

import jax
import jax.numpy as jnp
from jax import lax
from jax.experimental import pallas as pl
from jax.experimental.pallas import tpu as pltpu
from jax.sharding import PartitionSpec as P

VMEM_LIMIT = 61 * 1024 * 1024
F32, BF16 = jnp.float32, jnp.bfloat16
MESH = pl.DeviceIdType.MESH
LAG, DOWN_LAG, UP_LAG, END_LAG = 4, 2, 6, 2


def line_sizes(count):
    fast = 1
    while 4 * fast * fast <= count:
        fast *= 2
    return count // fast, fast


def tile(size, most):
    width = min(size, most)
    while size % width:
        width //= 2
    return width


def dequantized(codes, exponents):
    rows, columns = codes.shape
    scale = jnp.exp2(exponents.astype(F32)).astype(BF16)
    return (codes.reshape(rows // 32, 32, columns) * scale[:, None, :]).reshape(rows, columns)


class Plan:
    def __init__(self, slow, fast, tokens, columns, width):
        self.slow, self.fast, self.near = slow, fast, slow // 2
        self.tokens, self.total, self.columns, self.width = tokens, 2 * tokens, columns, width
        self.piece = tile(width, 512)
        self.parts = width // self.piece
        self.tiles = columns // self.piece
        self.cut = self.total * 19 // 32 // 16 * 16
        self.rows = (pl.ds(0, self.cut), pl.ds(self.cut, self.total - self.cut))

    def locate(self):
        grid, self.core = lax.axis_index("grid"), lax.axis_index("depth")
        self.y = grid % self.fast
        self.u = self.line(grid // self.fast)

    def line(self, place):
        return place + self.core * (self.slow - 1 - 2 * place)

    def grid_of(self, u, y):
        return self.line(u) * self.fast + y

    def index(self, owner, row, part):
        local = owner + self.core * (self.near - 1 - 2 * owner)
        return (local * self.fast + row) * self.parts + part

    def span(self, index):
        return pl.ds(pl.multiple_of(index * self.piece, self.piece), self.piece)

    def first_order(self, i):
        owner, rest = i // (self.fast * self.parts), i % (self.fast * self.parts)
        return owner, (self.y + 1 + rest // self.parts) % self.fast, rest % self.parts

    def second_order(self, i):
        step, rest = i // (self.fast * self.parts), i % (self.fast * self.parts)
        owner = (jnp.minimum(self.u, self.near - 1) - step + self.near) % self.near
        return owner, (self.y + rest // self.parts) % self.fast, rest % self.parts


def main_body(
    plan,
    gate_in,
    up_in,
    codes_in,
    exponents_in,
    cot_ref,
    hid_out,
    cot_out,
    grad_out,
    rows_out,
    hid,
    cots,
    part_sums,
    above,
    below,
    crossed,
    ended,
    sums,
    going,
    hid_send,
    hid_recv,
    hand_own,
    hand_send,
    hand_recv,
    gather_send,
    gather_recv,
    cross_send,
    cross_recv,
    end_send,
    end_recv,
    line_send,
    above_recv,
    below_recv,
    grad_send,
    grad_recv,
    rows_own,
    rows_send,
    rows_recv,
    save_sem,
    mine_sem,
    gate_ref,
    up_ref,
    codes_slots,
    exponents_slots,
    gate_sem,
    up_sem,
    codes_sem,
    exponents_sem,
    came,
):
    plan.locate()
    slow, fast, near, parts, tiles = plan.slow, plan.fast, plan.near, plan.parts, plan.tiles
    u, y, core, tokens = plan.u, plan.y, plan.core, plan.tokens
    step = pl.program_id(0)
    last = pl.num_programs(0) - 1
    units = hid.shape[1]
    own_rows = pl.ds(pl.multiple_of(core * tokens, tokens), tokens)
    other_rows = pl.ds(pl.multiple_of((1 - core) * tokens, tokens), tokens)

    def remote(source, target, send, recv, uu, yy, depth=None):
        place = plan.grid_of(uu, yy)
        return pltpu.make_async_remote_copy(
            src_ref=source,
            dst_ref=target,
            send_sem=send,
            recv_sem=recv,
            device_id={"grid": place, "depth": core if depth is None else depth},
            device_id_type=MESH,
        )

    def across_chip(source, target, send, recv):
        return pltpu.make_async_remote_copy(
            src_ref=source,
            dst_ref=target,
            send_sem=send,
            recv_sem=recv,
            device_id={"grid": lax.axis_index("grid"), "depth": 1 - core},
            device_id_type=MESH,
        )

    def wait_for(place, sem):
        pltpu.make_async_copy(place, place, sem).wait()

    def each(count, body):
        if count == 1:
            body(0)
        else:
            lax.fori_loop(0, count, lambda i, _: (body(i), 0)[1], 0)

    has_up, has_down = u < slow - 1, u > 0
    is_owner = u < near

    def code_copies(at):
        first = plan.index(*plan.first_order(jnp.minimum(at, tiles - 1)))
        second = plan.index(*plan.second_order(jnp.maximum(at - tiles, 0)))
        span = plan.span(jnp.where(at < tiles, first, second))
        slot = at % 2
        return (
            pltpu.make_async_copy(codes_in.at[:, span], codes_slots.at[slot], codes_sem.at[slot]),
            pltpu.make_async_copy(exponents_in.at[:, span], exponents_slots.at[slot], exponents_sem.at[slot]),
        )

    def fetch(at):
        for copy in code_copies(at):
            copy.start()

    def branch_copies(i):
        columns = pl.ds(pl.multiple_of(i * hid_width, hid_width), hid_width)
        return (
            pltpu.make_async_copy(gate_in.at[:, columns], gate_ref.at[:, columns], gate_sem.at[i]),
            pltpu.make_async_copy(up_in.at[:, columns], up_ref.at[:, columns], up_sem.at[i]),
        )

    hid_parts = hid_send.shape[0]
    hid_width = units // hid_parts
    codes_ref, exponents_ref = codes_slots.at[step % 2], exponents_slots.at[step % 2]

    def greet():
        barrier = pltpu.get_barrier_semaphore()

        def hail(grid, depth):
            pl.semaphore_signal(barrier, inc=1, device_id={"grid": grid, "depth": depth}, device_id_type=MESH)

        @pl.when(has_up)
        def _():
            hail(plan.grid_of(u + 1, y), core)

        @pl.when(has_down)
        def _():
            hail(plan.grid_of(u - 1, y), core)

        for turn in range(1, fast):
            hail(plan.grid_of(u, (y + turn) % fast), core)
        hail(lax.axis_index("grid"), 1 - core)
        count = fast + has_up.astype(jnp.int32) + has_down.astype(jnp.int32)
        pl.semaphore_wait(barrier, count)

    def hand_piece(part):
        return cot_ref.at[:, plan.span(part)]

    def hand_over(part):
        owner = slow - 1 - u
        place = cots.at[own_rows, plan.span(_far_index(owner, part))]
        return across_chip(hand_piece(part), place, hand_send.at[part], hand_recv.at[part])

    def _far_index(owner, part):
        local = owner + (1 - core) * (near - 1 - 2 * owner)
        return (local * fast + y) * parts + part

    def keep_own(part):
        place = cots.at[own_rows, plan.span(plan.index(u, y, part))]
        return pltpu.make_async_copy(hand_piece(part), place, hand_own.at[part])

    def start_hand_over():
        @pl.when(is_owner)
        def _():
            for part in range(parts):
                keep_own(part).start()

        @pl.when(jnp.logical_not(is_owner))
        def _():
            for part in range(parts):
                hand_over(part).start()

    def block(kind, owner, row, part):
        return cots.at[plan.rows[kind], plan.span(plan.index(owner, row, part))]

    def gather_copy(kind, owner, row, part, way):
        index = plan.index(owner, row, part)
        place = block(kind, owner, row, part)
        uu, yy = (u + 1, y) if way == 0 else (u - 1, y) if way == 1 else (u, (y + way - 1) % fast)
        return remote(place, place, gather_send.at[kind, index, way], gather_recv.at[kind, index], uu, yy)

    def gather_ways(kind, owner, row, part, act):
        @pl.when(jnp.logical_and(u >= owner, has_up))
        def _():
            act(gather_copy(kind, owner, row, part, 0))

        @pl.when(jnp.logical_and(u <= owner, has_down))
        def _():
            act(gather_copy(kind, owner, row, part, 1))

        def over():
            for turn in range(1, fast):
                act(gather_copy(kind, owner, row, part, 1 + turn))

        if kind == 0:
            over()
        else:
            pl.when(jnp.logical_and(u == owner, row == y))(over)

    def start(copy):
        copy.start()

    def send_own(part):
        @pl.when(is_owner)
        def _():
            keep_own(part).wait()
            wait_for(cots.at[other_rows, plan.span(plan.index(u, y, part))], hand_recv.at[part])
            gather_ways(1, u, y, part, start)
            gather_ways(0, u, y, part, start)

    def pass_on(kind, owner, row, part):
        wait_for(block(kind, owner, row, part), gather_recv.at[kind, plan.index(owner, row, part)])
        gather_ways(kind, owner, row, part, start)

    def pass_crossed(part):
        @pl.when(is_owner)
        def _():
            each(fast - 1, lambda turn: pass_on(1, u, (y + 1 + turn) % fast, part))

    def pass_round(hop, part):
        for owner in (u - hop, u + hop):

            @pl.when(jnp.logical_and(owner >= 0, owner < near))
            def _():
                pass_on(0, owner, y, part)
                each(fast, lambda turn: pass_on(1, owner, (y + turn) % fast, part))

    def finish_gather():
        @pl.when(jnp.logical_not(is_owner))
        def _():
            for part in range(parts):
                hand_over(part).wait_send()

        def one(i):
            owner, rest = i // (fast * parts), i % (fast * parts)
            row, part = rest // parts, rest % parts

            @pl.when(row == y)
            def _():
                gather_ways(0, owner, row, part, lambda copy: copy.wait_send())

            gather_ways(1, owner, row, part, lambda copy: copy.wait_send())

        each(tiles, one)

    def hid_copy(i):
        place = hid.at[own_rows, pl.ds(pl.multiple_of(i * hid_width, hid_width), hid_width)]
        return across_chip(place, place, hid_send.at[i], hid_recv.at[i])

    def make_hidden(first, count):
        def one(i):
            columns = pl.ds(pl.multiple_of(i * hid_width, hid_width), hid_width)
            strip = min(32, tokens)
            for copy in branch_copies(i):
                copy.wait()

            def few(k, _):
                rows = pl.ds(pl.multiple_of(k * strip, strip), strip)
                gate = gate_ref[rows, columns].astype(F32)
                value = gate * jax.nn.sigmoid(gate) * up_ref[rows, columns].astype(F32)
                hid[pl.ds(pl.multiple_of(core * tokens + k * strip, strip), strip), columns] = value.astype(BF16)
                return 0

            lax.fori_loop(0, tokens // strip, few, 0, unroll=min(4, tokens // strip))
            hid_copy(i).start()

        lax.fori_loop(first, first + count, lambda i, _: (one(i), 0)[1], 0)

    def hidden_arrives():
        def one(i):
            place = hid.at[other_rows, pl.ds(pl.multiple_of(i * hid_width, hid_width), hid_width)]
            wait_for(place, hid_recv.at[i])

        each(hid_parts, one)

    def out_piece(ref, kind, index):
        return ref.at[plan.rows[kind], plan.span(index)]

    def cross_place(owner, source, part):
        index = (source * near + owner) * parts + part
        return crossed.at[plan.rows[0], plan.span(index)], cross_recv.at[index]

    def cross_copy(owner, row, part):
        index = plan.index(owner, row, part)
        place, recv = cross_place(owner, y, part)
        return remote(out_piece(part_sums, 0, index), place, cross_send.at[index], recv, u, row)

    def end_place(source, part):
        index = source * parts + part
        return ended.at[:, plan.span(index)], end_recv.at[index]

    def end_copy(row, part):
        index = plan.index(u, row, part)
        place, recv = end_place(y, part)
        return remote(out_piece(part_sums, 1, index), place, end_send.at[index], recv, u, row)

    def line_copy(kind, owner, row, part, up):
        index = plan.index(owner, row, part)
        source = out_piece(part_sums, kind, index)
        if up:
            return remote(
                source, out_piece(below, kind, index), line_send.at[kind, index], below_recv.at[kind, index], u + 1, y
            )
        return remote(
            source, out_piece(above, kind, index), line_send.at[kind, index], above_recv.at[kind, index], u - 1, y
        )

    def combine(kind, index, places):
        for place, sem in places:
            wait_for(place, sem)
        target = out_piece(part_sums, kind, index)
        height = target.shape[0]
        strip = 32 if height % 32 == 0 else 16

        def few(k, _):
            rows = pl.ds(pl.multiple_of(k * strip, strip), strip)
            value = target[rows, :].astype(F32)
            for place, _ in places:
                value += place[rows, :].astype(F32)
            target[rows, :] = value.astype(BF16)
            return 0

        lax.fori_loop(0, height // strip, few, 0)

    def line_event(owner, row, part):
        index = plan.index(owner, row, part)

        def one(kind):
            crossing = [cross_place(owner, (y + turn) % fast, part) for turn in range(1, fast)] if kind == 0 else []
            from_above = out_piece(above, kind, index), above_recv.at[kind, index]
            from_below = out_piece(below, kind, index), below_recv.at[kind, index]
            takes_above = jnp.logical_and(u >= owner, has_up)
            takes_below = jnp.logical_and(u <= owner, has_down)

            @pl.when(jnp.logical_and(takes_above, takes_below))
            def _():
                combine(kind, index, [*crossing, from_above, from_below])

            @pl.when(jnp.logical_and(takes_above, jnp.logical_not(takes_below)))
            def _():
                combine(kind, index, [*crossing, from_above])

            @pl.when(jnp.logical_and(takes_below, jnp.logical_not(takes_above)))
            def _():
                combine(kind, index, [*crossing, from_below])

            if kind == 0:

                @pl.when(jnp.logical_not(jnp.logical_or(takes_above, takes_below)))
                def _():
                    combine(kind, index, crossing)

            @pl.when(u > owner)
            def _():
                line_copy(kind, owner, row, part, False).start()

            @pl.when(u < owner)
            def _():
                line_copy(kind, owner, row, part, True).start()

        pl.when(row == y)(lambda: one(0))
        one(1)

        @pl.when(jnp.logical_and(u == owner, row != y))
        def _():
            end_copy(row, part).start()

    def rows_copies(part):
        index = plan.index(u, y, part)
        target = rows_out.at[:, plan.span(part)]
        kept = pltpu.make_async_copy(part_sums.at[own_rows, plan.span(index)], target, rows_own.at[part])
        sent = across_chip(
            part_sums.at[other_rows, plan.span(index)], target, rows_send.at[part], rows_recv.at[part]
        )
        return kept, sent

    def final_event(row, part):
        @pl.when(row == y)
        def _():
            index = plan.index(u, y, part)
            combine(1, index, [end_place((y + turn) % fast, part) for turn in range(1, fast)])
            for copy in rows_copies(part):
                copy.start()

    def sum_events():
        down, up = DOWN_LAG + LAG * (slow - 1 - u), UP_LAG + LAG * u

        def at(lag, body):
            first = jnp.maximum(step - lag, 0)
            end = jnp.minimum(jnp.where(step == last, tiles, step - lag + 1), tiles)
            lax.fori_loop(first, end, lambda i, _: (body(*plan.first_order(i)), 0)[1], 0)

        at(up, lambda owner, row, part: pl.when(owner > u)(lambda: line_event(owner, row, part)))
        at(down, lambda owner, row, part: pl.when(owner <= u)(lambda: line_event(owner, row, part)))
        at(down + END_LAG, lambda owner, row, part: pl.when(owner == u)(lambda: final_event(row, part)))

    def finish_sums():
        def one(i):
            owner, rest = i // (fast * parts), i % (fast * parts)
            row, part = rest // parts, rest % parts

            @pl.when(row != y)
            def _():
                cross_copy(owner, row, part).wait_send()

            for kind in range(2):

                def sent(kind=kind):
                    line_copy(kind, owner, row, part, True).wait_send()

                moved = u != owner
                pl.when(jnp.logical_and(moved, row == y) if kind == 0 else moved)(sent)

            @pl.when(jnp.logical_and(u == owner, row != y))
            def _():
                end_copy(row, part).wait_send()

        each(tiles, one)

        @pl.when(is_owner)
        def _():
            for part in range(parts):
                kept, sent = rows_copies(part)
                kept.wait()
                sent.wait_send()

        @pl.when(jnp.logical_not(is_owner))
        def _():
            for part in range(parts):
                wait_for(rows_out.at[:, plan.span(part)], rows_recv.at[part])

    slices = grad_send.shape[0]
    slice_width = units // slices

    def slice_of(i):
        return pl.ds(i * slice_width, slice_width)

    def grad_copy(i):
        return across_chip(going.at[:, slice_of(i)], came.at[:, slice_of(i)], grad_send.at[i], grad_recv.at[i])

    def grad_save(i):
        return pltpu.make_async_copy(came.at[:, slice_of(i)], grad_out.at[:, slice_of(i)], mine_sem.at[i])

    def save(source, target, index):
        return pltpu.make_async_copy(source, target, save_sem.at[index])

    @pl.when(step == 0)
    def _():
        for i in range(hid_parts):
            for copy in branch_copies(i):
                copy.start()
        fetch(step)
        greet()
        start_hand_over()
        early = max(1, hid_parts // 8)
        make_hidden(0, early)
        for part in range(parts):
            send_own(part)
        make_hidden(early, hid_parts - early)
        hidden_arrives()
        save(hid, hid_out, 0).start()

    @pl.when(step == 1)
    def _():
        for part in range(parts):
            pass_crossed(part)

    @pl.when(step < last)
    def _():
        fetch(step + 1)

    whole = fast * parts
    for hop in range(1, slow):
        for part in range(parts):
            lead = slow - near
            if hop < lead:
                when = max(1, hop * tiles // lead - 1) + part
            else:
                when = tiles + (hop - lead) * whole - min(hop - lead, 1) + part

            @pl.when(step == when)
            def _():
                pass_round(hop, part)

    for copy in code_copies(step):
        copy.wait()

    @pl.when(step < tiles)
    def _():
        owner, row, part = plan.first_order(step)
        index = plan.index(owner, row, part)
        depth = tile(units, 1024)
        total = None
        for begin in range(0, units, depth):
            weight = dequantized(
                codes_ref[begin : begin + depth, :], exponents_ref[begin // 32 : (begin + depth) // 32, :]
            )
            term = jnp.dot(hid[:, begin : begin + depth], weight, preferred_element_type=F32)
            total = term if total is None else total + term
        part_sums[:, plan.span(index)] = total.astype(BF16)

        @pl.when(row != y)
        def _():
            cross_copy(owner, row, part).start()

    @pl.when(step >= tiles)
    def _():
        owner, row, part = plan.second_order(step - tiles)
        index = plan.index(owner, row, part)

        @pl.when(row != y)
        def _():
            wait_for(block(0, owner, row, part), gather_recv.at[0, index])

        def term_of(i):
            weight = dequantized(
                codes_ref[i * slice_width : (i + 1) * slice_width, :],
                exponents_ref[i * slice_width // 32 : (i + 1) * slice_width // 32, :],
            )
            return lax.dot_general(
                cots[:, plan.span(index)], weight, (((1,), (1,)), ((), ())), preferred_element_type=F32
            )

        @pl.when(step == tiles)
        def _():
            for i in range(slices):
                sums[:, slice_of(i)] = term_of(i)

        @pl.when(jnp.logical_and(step > tiles, step < last))
        def _():
            for i in range(slices):
                sums[:, slice_of(i)] += term_of(i)

        @pl.when(step == last)
        def _():
            save(cots, cot_out, 1).start()
            for i in range(slices):
                sums[:, slice_of(i)] += term_of(i)
                going[:, slice_of(i)] = sums[other_rows, slice_of(i)].astype(BF16)
                grad_copy(i).start()

    sum_events()

    @pl.when(step == last)
    def _():
        strip = min(32, tokens)
        for i in range(slices):
            grad_copy(i).wait_recv()

            def few(k, _):
                rows = pl.ds(pl.multiple_of(k * strip, strip), strip)
                own = pl.ds(pl.multiple_of(core * tokens + k * strip, strip), strip)
                value = sums[own, slice_of(i)] + came[rows, slice_of(i)].astype(F32)
                came[rows, slice_of(i)] = value.astype(BF16)
                return 0

            lax.fori_loop(0, tokens // strip, few, 0, unroll=min(4, tokens // strip))
            grad_save(i).start()
        for i in range(slices):
            grad_copy(i).wait_send()
            grad_save(i).wait()
        save(hid, hid_out, 0).wait()
        save(cots, cot_out, 1).wait()
        each(hid_parts, lambda i: hid_copy(i).wait_send())
        finish_gather()
        finish_sums()


def main_kernel(gate, up, codes, exponents, cotangent, slow, fast):
    tokens, units = gate.shape
    columns, width = codes.shape[1], cotangent.shape[1]
    plan = Plan(slow, fast, tokens, columns, width)
    tiles, parts, total, piece = plan.tiles, plan.parts, plan.total, plan.piece
    anywhere = pl.BlockSpec(memory_space=pl.ANY)
    dma = pltpu.SemaphoreType.DMA
    hid_parts = max(1, units // 512)
    slices = max(1, units // 512)

    return pl.pallas_call(
        functools.partial(main_body, plan),
        grid=(2 * tiles,),
        in_specs=[anywhere] * 5,
        out_specs=[anywhere] * 4,
        out_shape=[
            jax.ShapeDtypeStruct((total, units), BF16),
            jax.ShapeDtypeStruct((total, columns), BF16),
            jax.ShapeDtypeStruct((tokens, units), BF16),
            jax.ShapeDtypeStruct((tokens, width), BF16),
        ],
        scratch_shapes=[
            pltpu.VMEM((total, units), BF16),
            pltpu.VMEM((total, columns), BF16),
            pltpu.VMEM((total, columns), BF16),
            pltpu.VMEM((total, columns), BF16),
            pltpu.VMEM((total, columns), BF16),
            pltpu.VMEM((plan.cut, columns), BF16),
            pltpu.VMEM((total - plan.cut, fast * width), BF16),
            pltpu.VMEM((total, units), F32),
            pltpu.VMEM((tokens, units), BF16),
            dma((hid_parts,)),
            dma((hid_parts,)),
            dma((parts,)),
            dma((parts,)),
            dma((parts,)),
            dma((2, tiles, 1 + fast)),
            dma((2, tiles)),
            dma((tiles,)),
            dma((tiles,)),
            dma((tiles,)),
            dma((fast * parts,)),
            dma((2, tiles)),
            dma((2, tiles)),
            dma((2, tiles)),
            dma((slices,)),
            dma((slices,)),
            dma((parts,)),
            dma((parts,)),
            dma((parts,)),
            dma((2,)),
            dma((slices,)),
            pltpu.VMEM((tokens, units), BF16),
            pltpu.VMEM((tokens, units), BF16),
            pltpu.VMEM((2, units, piece), BF16),
            pltpu.VMEM((2, units // 32, piece), jnp.int32),
            dma((hid_parts,)),
            dma((hid_parts,)),
            dma((2,)),
            dma((2,)),
            pltpu.VMEM((tokens, units), BF16),
        ],
        compiler_params=pltpu.CompilerParams(
            vmem_limit_bytes=VMEM_LIMIT, collective_id=0, has_side_effects=True
        ),
        cost_estimate=pl.CostEstimate(
            flops=8 * tokens * units * columns, bytes_accessed=4 * units * columns, transcendentals=0
        ),
        name="main",
    )(gate, up, codes, exponents, cotangent)


def rest_body(
    width,
    gate_ref,
    up_ref,
    hid_ref,
    grad_ref,
    cot_in,
    rows_ref,
    grad_gate_ref,
    grad_up_ref,
    grad_weight_ref,
    rows_out_ref,
    cot,
    cot_sem,
):
    step = pl.program_id(0)
    parts = cot.shape[1] // width
    strip = gate_ref.shape[0] // parts

    def cot_copy(i):
        columns = pl.ds(i * width, width)
        return pltpu.make_async_copy(cot_in.at[:, columns], cot.at[:, columns], cot_sem.at[i])

    def work(before):
        left = hid_ref[...].T
        for i in range(parts):
            before(i)
            part = slice(i * strip, (i + 1) * strip)
            gate = gate_ref[part, :].astype(F32)
            sigmoid = jax.nn.sigmoid(gate)
            grad = grad_ref[part, :].astype(F32)
            slope = sigmoid * (1.0 + gate * (1.0 - sigmoid))
            grad_gate = (grad * up_ref[part, :].astype(F32) * slope).astype(BF16)
            grad_up = (grad * (gate * sigmoid)).astype(BF16)
            term = jnp.dot(left, cot[:, i * width : (i + 1) * width], preferred_element_type=F32)
            grad_weight_ref[:, i * width : (i + 1) * width] = term.astype(BF16)
            grad_gate_ref[part, :] = grad_gate
            grad_up_ref[part, :] = grad_up

    @pl.when(step == 0)
    def _():
        for i in range(parts):
            cot_copy(i).start()
        rows_out_ref[...] = rows_ref[...]
        work(lambda i: cot_copy(i).wait())

    @pl.when(step > 0)
    def _():
        work(lambda i: None)


def rest(gate, up, hidden, cot_all, grad, rows):
    total, units = hidden.shape
    tokens = gate.shape[0]
    columns = cot_all.shape[1]
    height, width = tile(units, 512), tile(columns, 1024)
    part = pl.BlockSpec((tokens, height), lambda i: (0, i))
    still = pl.BlockSpec(rows.shape, lambda i: (0, 0), pipeline_mode=pl.Buffered(1))
    return pl.pallas_call(
        functools.partial(rest_body, width),
        grid=(units // height,),
        in_specs=[
            part,
            part,
            pl.BlockSpec((total, height), lambda i: (0, i)),
            part,
            pl.BlockSpec(memory_space=pl.ANY),
            still,
        ],
        out_specs=[
            part,
            part,
            pl.BlockSpec((height, columns), lambda i: (i, 0)),
            pl.BlockSpec(rows.shape, lambda i: (0, 0)),
        ],
        out_shape=[
            jax.ShapeDtypeStruct((tokens, units), BF16),
            jax.ShapeDtypeStruct((tokens, units), BF16),
            jax.ShapeDtypeStruct((units, columns), BF16),
            jax.ShapeDtypeStruct(rows.shape, BF16),
        ],
        scratch_shapes=[
            pltpu.VMEM((total, columns), BF16),
            pltpu.SemaphoreType.DMA((columns // width,)),
        ],
        compiler_params=pltpu.CompilerParams(vmem_limit_bytes=VMEM_LIMIT),
        cost_estimate=pl.CostEstimate(
            flops=2 * total * units * columns, bytes_accessed=2 * units * columns, transcendentals=tokens * units
        ),
        name="rest",
    )(gate, up, hidden, grad, cot_all, rows)


def shards(slow, fast, gate_input, up_input, code_values, exponents, cotangent):
    hidden, cot_all, grad, rows = main_kernel(
        gate_input, up_input, code_values, exponents, cotangent, slow, fast
    )
    grad_gate, grad_up, grad_weight, output_rows = rest(gate_input, up_input, hidden, cot_all, grad, rows)
    return (output_rows, grad_gate, grad_up, grad_weight)


def solution(mesh):
    tokens_units = P(("parts", "depth"), "grid")
    weights = P("grid", "depth")
    slow, fast = line_sizes(mesh.shape["grid"])
    return jax.shard_map(
        functools.partial(shards, slow, fast),
        mesh=mesh,
        in_specs=(tokens_units, tokens_units, weights, weights, tokens_units),
        out_specs=(tokens_units, tokens_units, tokens_units, P(("parts", "grid"), "depth")),
        check_vma=False,
    )
```

```python
import functools

import jax
import jax.numpy as jnp
from jax import lax
from jax.experimental import pallas as pl
from jax.experimental.pallas import tpu as pltpu
from jax.sharding import PartitionSpec as P

VMEM_LIMIT = 52 * 1024 * 1024
F32, BF16 = jnp.float32, jnp.bfloat16
MESH = pl.DeviceIdType.MESH
LAG, DOWN_LAG, UP_LAG, END_LAG = 4, 2, 6, 2


def line_sizes(count):
    fast = 1
    while 4 * fast * fast <= count:
        fast *= 2
    return count // fast, fast


def tile(size, most):
    width = min(size, most)
    while size % width:
        width //= 2
    return width


def dequantized(codes, exponents):
    rows, columns = codes.shape
    scale = jnp.exp2(exponents.astype(F32)).astype(BF16)
    return (codes.reshape(rows // 32, 32, columns) * scale[:, None, :]).reshape(rows, columns)


class Plan:
    def __init__(self, slow, fast, tokens, columns, width):
        self.slow, self.fast, self.near = slow, fast, slow // 2
        self.tokens, self.total, self.columns, self.width = tokens, 2 * tokens, columns, width
        self.piece = tile(width, 512)
        self.parts = width // self.piece
        self.tiles = columns // self.piece
        self.cut = self.total * 19 // 32 // 16 * 16
        self.rows = (pl.ds(0, self.cut), pl.ds(self.cut, self.total - self.cut))

    def locate(self):
        grid, self.core = lax.axis_index("grid"), lax.axis_index("depth")
        self.y = grid % self.fast
        self.u = self.line(grid // self.fast)

    def line(self, place):
        return place + self.core * (self.slow - 1 - 2 * place)

    def grid_of(self, u, y):
        return self.line(u) * self.fast + y

    def index(self, owner, row, part):
        local = owner + self.core * (self.near - 1 - 2 * owner)
        return (local * self.fast + row) * self.parts + part

    def span(self, index):
        return pl.ds(pl.multiple_of(index * self.piece, self.piece), self.piece)

    def first_order(self, i):
        owner, rest = i // (self.fast * self.parts), i % (self.fast * self.parts)
        return owner, (self.y + 1 + rest // self.parts) % self.fast, rest % self.parts

    def second_order(self, i):
        step, rest = i // (self.fast * self.parts), i % (self.fast * self.parts)
        owner = (jnp.minimum(self.u, self.near - 1) - step + self.near) % self.near
        return owner, (self.y + rest // self.parts) % self.fast, rest % self.parts


def main_body(
    plan,
    gate_in,
    up_in,
    codes_in,
    exponents_in,
    cot_ref,
    hid_out,
    cot_out,
    grad_out,
    rows_out,
    hid,
    cots,
    part_sums,
    above,
    below,
    crossed,
    ended,
    sums,
    going,
    hid_send,
    hid_recv,
    hand_own,
    hand_send,
    hand_recv,
    gather_send,
    gather_recv,
    cross_send,
    cross_recv,
    end_send,
    end_recv,
    line_send,
    above_recv,
    below_recv,
    grad_send,
    grad_recv,
    rows_own,
    rows_send,
    rows_recv,
    save_sem,
    mine_sem,
    gate_ref,
    up_ref,
    codes_slots,
    exponents_slots,
    gate_sem,
    up_sem,
    codes_sem,
    exponents_sem,
    came,
):
    plan.locate()
    slow, fast, near, parts, tiles = plan.slow, plan.fast, plan.near, plan.parts, plan.tiles
    u, y, core, tokens = plan.u, plan.y, plan.core, plan.tokens
    step = pl.program_id(0)
    last = pl.num_programs(0) - 1
    units = hid.shape[1]
    own_rows = pl.ds(pl.multiple_of(core * tokens, tokens), tokens)
    other_rows = pl.ds(pl.multiple_of((1 - core) * tokens, tokens), tokens)

    def remote(source, target, send, recv, uu, yy, depth=None):
        place = plan.grid_of(uu, yy)
        return pltpu.make_async_remote_copy(
            src_ref=source,
            dst_ref=target,
            send_sem=send,
            recv_sem=recv,
            device_id={"grid": place, "depth": core if depth is None else depth},
            device_id_type=MESH,
        )

    def across_chip(source, target, send, recv):
        return pltpu.make_async_remote_copy(
            src_ref=source,
            dst_ref=target,
            send_sem=send,
            recv_sem=recv,
            device_id={"grid": lax.axis_index("grid"), "depth": 1 - core},
            device_id_type=MESH,
        )

    def wait_for(place, sem):
        pltpu.make_async_copy(place, place, sem).wait()

    def each(count, body):
        if count == 1:
            body(0)
        else:
            lax.fori_loop(0, count, lambda i, _: (body(i), 0)[1], 0)

    has_up, has_down = u < slow - 1, u > 0
    is_owner = u < near

    def code_copies(at):
        first = plan.index(*plan.first_order(jnp.minimum(at, tiles - 1)))
        second = plan.index(*plan.second_order(jnp.maximum(at - tiles, 0)))
        span = plan.span(jnp.where(at < tiles, first, second))
        slot = at % 2
        return (
            pltpu.make_async_copy(codes_in.at[:, span], codes_slots.at[slot], codes_sem.at[slot]),
            pltpu.make_async_copy(exponents_in.at[:, span], exponents_slots.at[slot], exponents_sem.at[slot]),
        )

    def fetch(at):
        for copy in code_copies(at):
            copy.start()

    def branch_copies(i):
        columns = pl.ds(pl.multiple_of(i * hid_width, hid_width), hid_width)
        return (
            pltpu.make_async_copy(gate_in.at[:, columns], gate_ref.at[:, columns], gate_sem.at[i]),
            pltpu.make_async_copy(up_in.at[:, columns], up_ref.at[:, columns], up_sem.at[i]),
        )

    hid_parts = hid_send.shape[0]
    hid_width = units // hid_parts
    codes_ref, exponents_ref = codes_slots.at[step % 2], exponents_slots.at[step % 2]

    def greet():
        barrier = pltpu.get_barrier_semaphore()

        def hail(grid, depth):
            pl.semaphore_signal(barrier, inc=1, device_id={"grid": grid, "depth": depth}, device_id_type=MESH)

        @pl.when(has_up)
        def _():
            hail(plan.grid_of(u + 1, y), core)

        @pl.when(has_down)
        def _():
            hail(plan.grid_of(u - 1, y), core)

        for turn in range(1, fast):
            hail(plan.grid_of(u, (y + turn) % fast), core)
        hail(lax.axis_index("grid"), 1 - core)
        count = fast + has_up.astype(jnp.int32) + has_down.astype(jnp.int32)
        pl.semaphore_wait(barrier, count)

    def hand_piece(part):
        return cot_ref.at[:, plan.span(part)]

    def hand_over(part):
        owner = slow - 1 - u
        place = cots.at[own_rows, plan.span(_far_index(owner, part))]
        return across_chip(hand_piece(part), place, hand_send.at[part], hand_recv.at[part])

    def _far_index(owner, part):
        local = owner + (1 - core) * (near - 1 - 2 * owner)
        return (local * fast + y) * parts + part

    def keep_own(part):
        place = cots.at[own_rows, plan.span(plan.index(u, y, part))]
        return pltpu.make_async_copy(hand_piece(part), place, hand_own.at[part])

    def start_hand_over():
        @pl.when(is_owner)
        def _():
            for part in range(parts):
                keep_own(part).start()

        @pl.when(jnp.logical_not(is_owner))
        def _():
            for part in range(parts):
                hand_over(part).start()

    def block(kind, owner, row, part):
        return cots.at[plan.rows[kind], plan.span(plan.index(owner, row, part))]

    def gather_copy(kind, owner, row, part, way):
        index = plan.index(owner, row, part)
        place = block(kind, owner, row, part)
        uu, yy = (u + 1, y) if way == 0 else (u - 1, y) if way == 1 else (u, (y + way - 1) % fast)
        return remote(place, place, gather_send.at[kind, index, way], gather_recv.at[kind, index], uu, yy)

    def gather_ways(kind, owner, row, part, act):
        @pl.when(jnp.logical_and(u >= owner, has_up))
        def _():
            act(gather_copy(kind, owner, row, part, 0))

        @pl.when(jnp.logical_and(u <= owner, has_down))
        def _():
            act(gather_copy(kind, owner, row, part, 1))

        def over():
            for turn in range(1, fast):
                act(gather_copy(kind, owner, row, part, 1 + turn))

        if kind == 0:
            over()
        else:
            pl.when(jnp.logical_and(u == owner, row == y))(over)

    def start(copy):
        copy.start()

    def send_own(part):
        @pl.when(is_owner)
        def _():
            keep_own(part).wait()
            wait_for(cots.at[other_rows, plan.span(plan.index(u, y, part))], hand_recv.at[part])
            gather_ways(1, u, y, part, start)
            gather_ways(0, u, y, part, start)

    def pass_on(kind, owner, row, part):
        wait_for(block(kind, owner, row, part), gather_recv.at[kind, plan.index(owner, row, part)])
        gather_ways(kind, owner, row, part, start)

    def pass_crossed(part):
        @pl.when(is_owner)
        def _():
            each(fast - 1, lambda turn: pass_on(1, u, (y + 1 + turn) % fast, part))

    def pass_round(hop, part):
        for owner in (u - hop, u + hop):

            @pl.when(jnp.logical_and(owner >= 0, owner < near))
            def _():
                pass_on(0, owner, y, part)
                each(fast, lambda turn: pass_on(1, owner, (y + turn) % fast, part))

    def finish_gather():
        @pl.when(jnp.logical_not(is_owner))
        def _():
            for part in range(parts):
                hand_over(part).wait_send()

        def one(i):
            owner, rest = i // (fast * parts), i % (fast * parts)
            row, part = rest // parts, rest % parts

            @pl.when(row == y)
            def _():
                gather_ways(0, owner, row, part, lambda copy: copy.wait_send())

            gather_ways(1, owner, row, part, lambda copy: copy.wait_send())

        each(tiles, one)

    def hid_copy(i):
        place = hid.at[own_rows, pl.ds(pl.multiple_of(i * hid_width, hid_width), hid_width)]
        return across_chip(place, place, hid_send.at[i], hid_recv.at[i])

    def make_hidden(first, count):
        def one(i):
            columns = pl.ds(pl.multiple_of(i * hid_width, hid_width), hid_width)
            strip = min(32, tokens)
            for copy in branch_copies(i):
                copy.wait()

            def few(k, _):
                rows = pl.ds(pl.multiple_of(k * strip, strip), strip)
                gate = gate_ref[rows, columns].astype(F32)
                value = gate * jax.nn.sigmoid(gate) * up_ref[rows, columns].astype(F32)
                hid[pl.ds(pl.multiple_of(core * tokens + k * strip, strip), strip), columns] = value.astype(BF16)
                return 0

            lax.fori_loop(0, tokens // strip, few, 0, unroll=min(4, tokens // strip))
            hid_copy(i).start()

        lax.fori_loop(first, first + count, lambda i, _: (one(i), 0)[1], 0)

    def hidden_arrives():
        def one(i):
            place = hid.at[other_rows, pl.ds(pl.multiple_of(i * hid_width, hid_width), hid_width)]
            wait_for(place, hid_recv.at[i])

        each(hid_parts, one)

    def out_piece(ref, kind, index):
        return ref.at[plan.rows[kind], plan.span(index)]

    def cross_place(owner, source, part):
        index = (source * near + owner) * parts + part
        return crossed.at[plan.rows[0], plan.span(index)], cross_recv.at[index]

    def cross_copy(owner, row, part):
        index = plan.index(owner, row, part)
        place, recv = cross_place(owner, y, part)
        return remote(out_piece(part_sums, 0, index), place, cross_send.at[index], recv, u, row)

    def end_place(source, part):
        index = source * parts + part
        return ended.at[:, plan.span(index)], end_recv.at[index]

    def end_copy(row, part):
        index = plan.index(u, row, part)
        place, recv = end_place(y, part)
        return remote(out_piece(part_sums, 1, index), place, end_send.at[index], recv, u, row)

    def line_copy(kind, owner, row, part, up):
        index = plan.index(owner, row, part)
        source = out_piece(part_sums, kind, index)
        if up:
            return remote(
                source, out_piece(below, kind, index), line_send.at[kind, index], below_recv.at[kind, index], u + 1, y
            )
        return remote(
            source, out_piece(above, kind, index), line_send.at[kind, index], above_recv.at[kind, index], u - 1, y
        )

    def combine(kind, index, places):
        for place, sem in places:
            wait_for(place, sem)
        target = out_piece(part_sums, kind, index)
        height = target.shape[0]
        strip = 32 if height % 32 == 0 else 16

        def few(k, _):
            rows = pl.ds(pl.multiple_of(k * strip, strip), strip)
            value = target[rows, :].astype(F32)
            for place, _ in places:
                value += place[rows, :].astype(F32)
            target[rows, :] = value.astype(BF16)
            return 0

        lax.fori_loop(0, height // strip, few, 0)

    def line_event(owner, row, part):
        index = plan.index(owner, row, part)

        def one(kind):
            crossing = [cross_place(owner, (y + turn) % fast, part) for turn in range(1, fast)] if kind == 0 else []
            from_above = out_piece(above, kind, index), above_recv.at[kind, index]
            from_below = out_piece(below, kind, index), below_recv.at[kind, index]
            takes_above = jnp.logical_and(u >= owner, has_up)
            takes_below = jnp.logical_and(u <= owner, has_down)

            @pl.when(jnp.logical_and(takes_above, takes_below))
            def _():
                combine(kind, index, [*crossing, from_above, from_below])

            @pl.when(jnp.logical_and(takes_above, jnp.logical_not(takes_below)))
            def _():
                combine(kind, index, [*crossing, from_above])

            @pl.when(jnp.logical_and(takes_below, jnp.logical_not(takes_above)))
            def _():
                combine(kind, index, [*crossing, from_below])

            if kind == 0:

                @pl.when(jnp.logical_not(jnp.logical_or(takes_above, takes_below)))
                def _():
                    combine(kind, index, crossing)

            @pl.when(u > owner)
            def _():
                line_copy(kind, owner, row, part, False).start()

            @pl.when(u < owner)
            def _():
                line_copy(kind, owner, row, part, True).start()

        pl.when(row == y)(lambda: one(0))
        one(1)

        @pl.when(jnp.logical_and(u == owner, row != y))
        def _():
            end_copy(row, part).start()

    def rows_copies(part):
        index = plan.index(u, y, part)
        target = rows_out.at[:, plan.span(part)]
        kept = pltpu.make_async_copy(part_sums.at[own_rows, plan.span(index)], target, rows_own.at[part])
        sent = across_chip(
            part_sums.at[other_rows, plan.span(index)], target, rows_send.at[part], rows_recv.at[part]
        )
        return kept, sent

    def final_event(row, part):
        @pl.when(row == y)
        def _():
            index = plan.index(u, y, part)
            combine(1, index, [end_place((y + turn) % fast, part) for turn in range(1, fast)])
            for copy in rows_copies(part):
                copy.start()

    def sum_events():
        down, up = DOWN_LAG + LAG * (slow - 1 - u), UP_LAG + LAG * u

        def at(lag, body):
            first = jnp.maximum(step - lag, 0)
            end = jnp.minimum(jnp.where(step == last, tiles, step - lag + 1), tiles)
            lax.fori_loop(first, end, lambda i, _: (body(*plan.first_order(i)), 0)[1], 0)

        at(up, lambda owner, row, part: pl.when(owner > u)(lambda: line_event(owner, row, part)))
        at(down, lambda owner, row, part: pl.when(owner <= u)(lambda: line_event(owner, row, part)))
        at(down + END_LAG, lambda owner, row, part: pl.when(owner == u)(lambda: final_event(row, part)))

    def finish_sums():
        def one(i):
            owner, rest = i // (fast * parts), i % (fast * parts)
            row, part = rest // parts, rest % parts

            @pl.when(row != y)
            def _():
                cross_copy(owner, row, part).wait_send()

            for kind in range(2):

                def sent(kind=kind):
                    line_copy(kind, owner, row, part, True).wait_send()

                moved = u != owner
                pl.when(jnp.logical_and(moved, row == y) if kind == 0 else moved)(sent)

            @pl.when(jnp.logical_and(u == owner, row != y))
            def _():
                end_copy(row, part).wait_send()

        each(tiles, one)

        @pl.when(is_owner)
        def _():
            for part in range(parts):
                kept, sent = rows_copies(part)
                kept.wait()
                sent.wait_send()

        @pl.when(jnp.logical_not(is_owner))
        def _():
            for part in range(parts):
                wait_for(rows_out.at[:, plan.span(part)], rows_recv.at[part])

    slices = grad_send.shape[0]
    slice_width = units // slices

    def slice_of(i):
        return pl.ds(i * slice_width, slice_width)

    def grad_copy(i):
        return across_chip(going.at[:, slice_of(i)], came.at[:, slice_of(i)], grad_send.at[i], grad_recv.at[i])

    def grad_save(i):
        return pltpu.make_async_copy(came.at[:, slice_of(i)], grad_out.at[:, slice_of(i)], mine_sem.at[i])

    def save(source, target, index):
        return pltpu.make_async_copy(source, target, save_sem.at[index])

    @pl.when(step == 0)
    def _():
        for i in range(hid_parts):
            for copy in branch_copies(i):
                copy.start()
        fetch(step)
        greet()
        start_hand_over()
        early = max(1, hid_parts // 8)
        make_hidden(0, early)
        for part in range(parts):
            send_own(part)
        make_hidden(early, hid_parts - early)
        hidden_arrives()
        save(hid, hid_out, 0).start()

    @pl.when(step == 1)
    def _():
        for part in range(parts):
            pass_crossed(part)

    @pl.when(step < last)
    def _():
        fetch(step + 1)

    whole = fast * parts
    for hop in range(1, slow):
        for part in range(parts):
            lead = slow - near
            if hop < lead:
                when = max(1, hop * tiles // lead - 1) + part
            else:
                when = tiles + (hop - lead) * whole - min(hop - lead, 1) + part

            @pl.when(step == when)
            def _():
                pass_round(hop, part)

    for copy in code_copies(step):
        copy.wait()

    @pl.when(step < tiles)
    def _():
        owner, row, part = plan.first_order(step)
        index = plan.index(owner, row, part)
        depth = tile(units, 1024)
        total = None
        for begin in range(0, units, depth):
            weight = dequantized(
                codes_ref[begin : begin + depth, :], exponents_ref[begin // 32 : (begin + depth) // 32, :]
            )
            term = jnp.dot(hid[:, begin : begin + depth], weight, preferred_element_type=F32)
            total = term if total is None else total + term
        part_sums[:, plan.span(index)] = total.astype(BF16)

        @pl.when(row != y)
        def _():
            cross_copy(owner, row, part).start()

    @pl.when(step >= tiles)
    def _():
        owner, row, part = plan.second_order(step - tiles)
        index = plan.index(owner, row, part)

        @pl.when(row != y)
        def _():
            wait_for(block(0, owner, row, part), gather_recv.at[0, index])

        def term_of(i):
            weight = dequantized(
                codes_ref[i * slice_width : (i + 1) * slice_width, :],
                exponents_ref[i * slice_width // 32 : (i + 1) * slice_width // 32, :],
            )
            return lax.dot_general(
                cots[:, plan.span(index)], weight, (((1,), (1,)), ((), ())), preferred_element_type=F32
            )

        @pl.when(step == tiles)
        def _():
            for i in range(slices):
                sums[:, slice_of(i)] = term_of(i)

        @pl.when(jnp.logical_and(step > tiles, step < last))
        def _():
            for i in range(slices):
                sums[:, slice_of(i)] += term_of(i)

        @pl.when(step == last)
        def _():
            save(cots, cot_out, 1).start()
            for i in range(slices):
                sums[:, slice_of(i)] += term_of(i)
                going[:, slice_of(i)] = sums[other_rows, slice_of(i)].astype(BF16)
                grad_copy(i).start()

    sum_events()

    @pl.when(step == last)
    def _():
        strip = min(32, tokens)
        for i in range(slices):
            grad_copy(i).wait_recv()

            def few(k, _):
                rows = pl.ds(pl.multiple_of(k * strip, strip), strip)
                own = pl.ds(pl.multiple_of(core * tokens + k * strip, strip), strip)
                value = sums[own, slice_of(i)] + came[rows, slice_of(i)].astype(F32)
                came[rows, slice_of(i)] = value.astype(BF16)
                return 0

            lax.fori_loop(0, tokens // strip, few, 0, unroll=min(4, tokens // strip))
            grad_save(i).start()
        for i in range(slices):
            grad_copy(i).wait_send()
            grad_save(i).wait()
        save(hid, hid_out, 0).wait()
        save(cots, cot_out, 1).wait()
        each(hid_parts, lambda i: hid_copy(i).wait_send())
        finish_gather()
        finish_sums()


def main_kernel(gate, up, codes, exponents, cotangent, slow, fast):
    tokens, units = gate.shape
    columns, width = codes.shape[1], cotangent.shape[1]
    plan = Plan(slow, fast, tokens, columns, width)
    tiles, parts, total, piece = plan.tiles, plan.parts, plan.total, plan.piece
    anywhere = pl.BlockSpec(memory_space=pl.ANY)
    dma = pltpu.SemaphoreType.DMA
    hid_parts = max(1, units // 512)
    slices = max(1, units // 512)

    return pl.pallas_call(
        functools.partial(main_body, plan),
        grid=(2 * tiles,),
        in_specs=[anywhere] * 5,
        out_specs=[anywhere] * 4,
        out_shape=[
            jax.ShapeDtypeStruct((total, units), BF16),
            jax.ShapeDtypeStruct((total, columns), BF16),
            jax.ShapeDtypeStruct((tokens, units), BF16),
            jax.ShapeDtypeStruct((tokens, width), BF16),
        ],
        scratch_shapes=[
            pltpu.VMEM((total, units), BF16),
            pltpu.VMEM((total, columns), BF16),
            pltpu.VMEM((total, columns), BF16),
            pltpu.VMEM((total, columns), BF16),
            pltpu.VMEM((total, columns), BF16),
            pltpu.VMEM((plan.cut, columns), BF16),
            pltpu.VMEM((total - plan.cut, fast * width), BF16),
            pltpu.VMEM((total, units), F32),
            pltpu.VMEM((tokens, units), BF16),
            dma((hid_parts,)),
            dma((hid_parts,)),
            dma((parts,)),
            dma((parts,)),
            dma((parts,)),
            dma((2, tiles, 1 + fast)),
            dma((2, tiles)),
            dma((tiles,)),
            dma((tiles,)),
            dma((tiles,)),
            dma((fast * parts,)),
            dma((2, tiles)),
            dma((2, tiles)),
            dma((2, tiles)),
            dma((slices,)),
            dma((slices,)),
            dma((parts,)),
            dma((parts,)),
            dma((parts,)),
            dma((2,)),
            dma((slices,)),
            pltpu.VMEM((tokens, units), BF16),
            pltpu.VMEM((tokens, units), BF16),
            pltpu.VMEM((2, units, piece), BF16),
            pltpu.VMEM((2, units // 32, piece), jnp.int32),
            dma((hid_parts,)),
            dma((hid_parts,)),
            dma((2,)),
            dma((2,)),
            pltpu.VMEM((tokens, units), BF16),
        ],
        compiler_params=pltpu.CompilerParams(
            vmem_limit_bytes=VMEM_LIMIT, collective_id=0, has_side_effects=True
        ),
        cost_estimate=pl.CostEstimate(
            flops=8 * tokens * units * columns, bytes_accessed=4 * units * columns, transcendentals=0
        ),
        name="main",
    )(gate, up, codes, exponents, cotangent)


def rest_body(
    width,
    gate_ref,
    up_ref,
    hid_ref,
    grad_ref,
    cot_in,
    rows_ref,
    grad_gate_ref,
    grad_up_ref,
    grad_weight_ref,
    rows_out_ref,
    cot,
    cot_sem,
):
    step = pl.program_id(0)
    parts = cot.shape[1] // width
    strip = gate_ref.shape[0] // parts

    def cot_copy(i):
        columns = pl.ds(i * width, width)
        return pltpu.make_async_copy(cot_in.at[:, columns], cot.at[:, columns], cot_sem.at[i])

    def work(before):
        left = hid_ref[...].T
        for i in range(parts):
            before(i)
            part = slice(i * strip, (i + 1) * strip)
            gate = gate_ref[part, :].astype(F32)
            sigmoid = jax.nn.sigmoid(gate)
            grad = grad_ref[part, :].astype(F32)
            slope = sigmoid * (1.0 + gate * (1.0 - sigmoid))
            grad_gate = (grad * up_ref[part, :].astype(F32) * slope).astype(BF16)
            grad_up = (grad * (gate * sigmoid)).astype(BF16)
            term = jnp.dot(left, cot[:, i * width : (i + 1) * width], preferred_element_type=F32)
            grad_weight_ref[:, i * width : (i + 1) * width] = term.astype(BF16)
            grad_gate_ref[part, :] = grad_gate
            grad_up_ref[part, :] = grad_up

    @pl.when(step == 0)
    def _():
        for i in range(parts):
            cot_copy(i).start()
        rows_out_ref[...] = rows_ref[...]
        work(lambda i: cot_copy(i).wait())

    @pl.when(step > 0)
    def _():
        work(lambda i: None)


def rest(gate, up, hidden, cot_all, grad, rows):
    total, units = hidden.shape
    tokens = gate.shape[0]
    columns = cot_all.shape[1]
    height, width = tile(units, 512), tile(columns, 1024)
    part = pl.BlockSpec((tokens, height), lambda i: (0, i))
    still = pl.BlockSpec(rows.shape, lambda i: (0, 0), pipeline_mode=pl.Buffered(1))
    return pl.pallas_call(
        functools.partial(rest_body, width),
        grid=(units // height,),
        in_specs=[
            part,
            part,
            pl.BlockSpec((total, height), lambda i: (0, i)),
            part,
            pl.BlockSpec(memory_space=pl.ANY),
            still,
        ],
        out_specs=[
            part,
            part,
            pl.BlockSpec((height, columns), lambda i: (i, 0)),
            pl.BlockSpec(rows.shape, lambda i: (0, 0)),
        ],
        out_shape=[
            jax.ShapeDtypeStruct((tokens, units), BF16),
            jax.ShapeDtypeStruct((tokens, units), BF16),
            jax.ShapeDtypeStruct((units, columns), BF16),
            jax.ShapeDtypeStruct(rows.shape, BF16),
        ],
        scratch_shapes=[
            pltpu.VMEM((total, columns), BF16),
            pltpu.SemaphoreType.DMA((columns // width,)),
        ],
        compiler_params=pltpu.CompilerParams(vmem_limit_bytes=VMEM_LIMIT),
        cost_estimate=pl.CostEstimate(
            flops=2 * total * units * columns, bytes_accessed=2 * units * columns, transcendentals=tokens * units
        ),
        name="rest",
    )(gate, up, hidden, grad, cot_all, rows)


def shards(slow, fast, gate_input, up_input, code_values, exponents, cotangent):
    hidden, cot_all, grad, rows = main_kernel(
        gate_input, up_input, code_values, exponents, cotangent, slow, fast
    )
    grad_gate, grad_up, grad_weight, output_rows = rest(gate_input, up_input, hidden, cot_all, grad, rows)
    return (output_rows, grad_gate, grad_up, grad_weight)


def solution(mesh):
    tokens_units = P(("parts", "depth"), "grid")
    weights = P("grid", "depth")
    slow, fast = line_sizes(mesh.shape["grid"])
    return jax.shard_map(
        functools.partial(shards, slow, fast),
        mesh=mesh,
        in_specs=(tokens_units, tokens_units, weights, weights, tokens_units),
        out_specs=(tokens_units, tokens_units, tokens_units, P(("parts", "grid"), "depth")),
        check_vma=False,
    )
```
